32 devices in a mesh: inst: 2 (over y), cell: 16 (over z, x, core).
Axes of the slice: x: 2, y: 2, z: 4, core: 2. Of those that a mesh axis runs over, the one named last changes fastest.
Arguments:
- adjoint: bfloat16 [4, 5, 32, 16, 256], P('inst', None, 'cell'), may hold values from -6 to 6
- flux_jac: bfloat16 [4, 5, 3, 32, 16, 256], P('inst', None, None, 'cell'), may hold values from -1.25 to 1.25
- shift: float32 [32, 16, 256], P('cell', 'inst'), may hold values from 0.1 to 2
Outputs:
- mesh_adjoint: float32 [3, 32, 16, 256], P(None, 'cell', 'inst')
- residual: float32 [3, 32, 16, 256], P(None, 'cell', 'inst')
The draws below stay inside these ranges and needn't reach their ends.
All inputs are finite; a program needn't handle non-finite values.
Results may differ from the reference program's by a relative error of at most 0.0003.
Values may be sent and summed in bfloat16 or wider, within the bound.
A program may use at most 64 MiB of HBM per device.

```python
import math
import jax
import jax.numpy as jnp
from jax import lax

NV = 5
NC = 3
ITERS = 3
NZ = 256
INSTANCES = 4
NX = 32
NY = 16


def strengthened(entries, key, source, target, parts, factor):
    owner, partner = [(jnp.arange(entries.shape[axis_at]) // (entries.shape[axis_at] // parts)).reshape([-1 if axis == axis_at else 1 for axis in range(entries.ndim)]) for axis_at in (source, target)]
    chosen = jax.random.permutation(key, parts)[partner]
    strong = (owner == chosen) | (owner == (partner + parts // 2) % parts)
    return jnp.where(strong, factor * entries, entries)


def steps_of(key, extent, cuts, low, top_value):
    gain = 1.0
    for axis_at, blocks in cuts:
        steps = jax.random.uniform(jax.random.fold_in(jax.random.fold_in(key, 6), axis_at), (blocks,), jnp.float32, low / len(cuts), top_value / len(cuts))
        gain = gain * jnp.repeat(jnp.exp(steps), extent[axis_at] // blocks).reshape((-1,) + (1,) * (len(extent) - 1 - axis_at))
    return gain


def bell_draw(key, shape, spread, reach, split=(), kind=jnp.bfloat16):
    drawn = jax.random.normal(key, shape, jnp.float32) * spread
    if len(split) > 0:
        drawn = steps_of(key, shape, split, -0.22, 0.18) * drawn
    return jnp.clip(drawn, min=-reach, max=reach).astype(kind)


def heavy_noise(rng, extent, spread, reach, split, heavy, dtype=jnp.bfloat16):
    array = spread * jax.random.normal(rng, extent, jnp.float32)
    if split:
        array = array * steps_of(rng, extent, split, -0.22, 0.18)
    return jnp.clip(strengthened(array, jax.random.fold_in(rng, 3), *heavy), -reach, reach).astype(dtype)


def setup_inputs(seed: int = 0) -> dict:
    splits = jax.random.split(jax.random.key(seed), 4)
    return {
        "adjoint": bell_draw(splits[0], (INSTANCES, NV, NX, NY, NZ), 1.0, 6.0, ((0, 2), (2, 16))),
        "flux_jac": heavy_noise(splits[1], (INSTANCES, NV, NC, NX, NY, NZ), (2 * NV * INSTANCES) ** -0.5, 1.25, ((0, 2), (3, 16)), (0, 4, 2, 2.0)),
        "shift": jnp.clip(jnp.exp(math.log(2.0) - 2.9957323 * jax.random.uniform(splits[2], (NX, NY, NZ), jnp.float32) ** steps_of(splits[2], (NX, NY, NZ), ((0, 16), (1, 2)), -0.2, 0.2)), 0.1, 2.0),
    }


mu_shear = 1.0
lame_first = 1.5


def instance_term(total, pair):
    adjoint_one, flux_one = pair
    padded = jnp.pad(adjoint_one.astype(jnp.float32), ((0, 0), (1, 1), (0, 0), (0, 0)))
    flux_full = flux_one.astype(jnp.float32)
    upper = jnp.einsum("vkxyz,vxyz->kxyz", flux_full, padded[:, 2:], precision=lax.Precision.HIGHEST)
    lower = jnp.einsum("vkxyz,vxyz->kxyz", flux_full, padded[:, :-2], precision=lax.Precision.HIGHEST)
    return total + (upper - lower), None


def operate(field, shift):
    padded = jnp.pad(field, ((0, 0), (1, 1), (1, 1), (1, 1)))
    beside = padded[:, 2:, 1:-1, 1:-1] + padded[:, :-2, 1:-1, 1:-1]
    beside = beside + padded[:, 1:-1, 2:, 1:-1] + padded[:, 1:-1, :-2, 1:-1]
    beside = beside + padded[:, 1:-1, 1:-1, 2:] + padded[:, 1:-1, 1:-1, :-2]
    diverge = (padded[0, 2:, 1:-1, 1:-1] - field[0]) + (padded[1, 1:-1, 2:, 1:-1] - field[1]) + (padded[2, 1:-1, 1:-1, 2:] - field[2])
    low_pad = jnp.pad(diverge, ((1, 0), (1, 0), (1, 0)))
    grad_part = jnp.stack([low_pad[:-1, 1:, 1:] - diverge, low_pad[1:, :-1, 1:] - diverge, low_pad[1:, 1:, :-1] - diverge])
    return mu_shear * (6.0 * field - beside) + shift * field + lame_first * grad_part


def reference(adjoint, flux_jac, shift):
    start = jnp.zeros((NC, NX, NY, NZ), jnp.float32)
    sens, _ = lax.scan(instance_term, start, (adjoint, flux_jac))
    mesh_adjoint = jnp.zeros_like(sens)
    residual, direction = sens, sens
    norm_now = jnp.sum(residual * residual)
    for sweep in range(ITERS):
        image = operate(direction, shift)
        alpha = norm_now / jnp.sum(direction * image)
        mesh_adjoint = mesh_adjoint + alpha * direction
        residual = residual - alpha * image
        norm_next = jnp.sum(residual * residual)
        direction = residual + (norm_next / norm_now) * direction
        norm_now = norm_next
    return mesh_adjoint, residual
```

```python
import functools

import jax
import jax.numpy as jnp
from jax import lax
from jax.experimental import pallas as pl
from jax.experimental.pallas import tpu as pltpu
from jax.sharding import PartitionSpec as P

ITERS = 3
LAME = 1.5
CENTER = 10.0
SPREAD = 8.0
HALO = 3
VMEM_GRANT = 40 << 20
MESH = pl.DeviceIdType.MESH
F32 = jnp.float32

ROW_A, ROW_B, ROW_C, ROW_D = 3, 4, 5, 6
PAIR_ROWS = (ROW_A, ROW_B, ROW_C, ROW_D)


def remote(src, dst, send_sem, recv_sem, device):
    return pltpu.make_async_remote_copy(
        src_ref=src,
        dst_ref=dst,
        send_sem=send_sem,
        recv_sem=recv_sem,
        device_id=device,
        device_id_type=MESH,
    )


def apply_operator(src, dst, sh, rows, valid_row, edges):
    y_first, y_last, z_first, z_last = edges
    wy, nz = src.shape[2], src.shape[3]

    def up_y(v):
        return jnp.where(y_last, 0.0, pltpu.roll(v, wy - 1, 0))

    def down_y(v):
        return jnp.where(y_first, 0.0, pltpu.roll(v, 1, 0))

    def up_z(v):
        return jnp.where(z_last, 0.0, pltpu.roll(v, nz - 1, 1))

    def down_z(v):
        return jnp.where(z_first, 0.0, pltpu.roll(v, 1, 1))

    def divergence(row):
        fields = [src[k, row] for k in range(3)]
        uy, uz = up_y(fields[1]), up_z(fields[2])
        dv = (src[0, row + 1] - fields[0]) + (uy - fields[1]) + (uz - fields[2])
        return fields, uy, uz, jnp.where(valid_row(row), dv, 0.0)

    before = {}
    for row in rows:
        if row - 1 not in before:
            before[row - 1] = divergence(row - 1)[3]
        fields, uy, uz, dv = divergence(row)
        before[row] = dv
        diag = sh[row - 1] + (6.0 - CENTER)
        shifted = [before[row - 1], down_y(dv), down_z(dv)]
        for k in range(3):
            u = fields[k]
            beside = src[k, row - 1] + src[k, row + 1]
            beside = beside + (uy if k == 1 else up_y(u)) + down_y(u)
            beside = beside + (uz if k == 2 else up_z(u)) + down_z(u)
            out = (diag * u - beside + LAME * (shifted[k] - dv)) * (1.0 / SPREAD)
            dst[k, row] = jnp.where(valid_row(row), out, 0.0)


def energy(src, sh, edges):
    _, y_last, _, z_last = edges
    wy, nz = src.shape[2], src.shape[3]
    total = None
    for row in PAIR_ROWS:
        dv = None
        for k in range(3):
            v = src[k, row]
            above = (
                src[k, row + 1],
                jnp.where(y_last, 0.0, pltpu.roll(v, wy - 1, 0)),
                jnp.where(z_last, 0.0, pltpu.roll(v, nz - 1, 1)),
            )
            step = above[k] - v
            dv = step if dv is None else dv + step
            diag = sh[row - 1] + (6.0 - CENTER)
            term = v * (diag * v - 2.0 * (above[0] + above[1] + above[2]))
            total = term if total is None else total + term
        total = total + LAME * (dv * dv)
    return total * (1.0 / SPREAD)


def coefficients(mu):
    def inner(a, b, skip=0):
        total = None
        for p, x in enumerate(a):
            for q, y in enumerate(b):
                if x is None or y is None:
                    continue
                term = x * y * mu[p + q]
                total = term if total is None else total + term
        return total

    def times(a):
        return [
            (CENTER * a[j] if j < len(a) else 0.0) + (SPREAD * a[j - 1] if j > 0 else 0.0)
            for j in range(len(a) + 1)
        ]

    one = jnp.ones_like(mu[0])
    solution_at, residual, direction = [], [one], [one]
    norm_now = mu[0]
    for sweep in range(ITERS):
        image = times(direction)
        alpha = norm_now / inner(direction, image)
        solution_at = [
            (solution_at[j] if j < len(solution_at) else 0.0) + alpha * direction[j]
            for j in range(len(direction))
        ]
        residual = [
            (residual[j] if j < len(residual) else 0.0) - alpha * image[j]
            for j in range(len(image))
        ]
        if sweep + 1 < ITERS:
            norm_next = inner(residual, residual)
            ratio = norm_next / norm_now
            direction = [
                residual[j] + (ratio * direction[j] if j < len(direction) else 0.0)
                for j in range(len(residual))
            ]
            norm_now = norm_next
    return solution_at, residual


def kernel(
    n_inst, n_cell, cols, window,
    adj_hbm, flux_hbm, shift_hbm, x_ref, r_ref,
    adj, flux, part, got, u0, u1, u2, u3, sh, basis, pack, gath, pack2, gath2,
    load_sem, give_send, give_recv, halo_send, halo_recv, sh_send, sh_recv,
    y_send, y_recv, in_send, in_recv, x_send, x_recv, b_send, b_recv,
    g_send, g_recv, h_send, h_recv, near,
):
    i, c = lax.axis_index("inst"), lax.axis_index("cell")
    n_pair = n_cell // 2
    m = c // 2
    wy = window * cols
    n_v = adj.shape[1]
    nv = adj.shape[0] * n_v
    ny, nz = adj.shape[3], adj.shape[4]
    halves = 2 if nz % 256 == 0 else 1
    split = window < n_inst
    has_prev, has_next = m > 0, m < n_pair - 1
    barrier = pltpu.get_barrier_semaphore()

    def lanes(h):
        return slice(h * (nz // halves), (h + 1) * (nz // halves))

    def start_of(j):
        return jnp.clip(j - 1, 0, n_inst - window)

    def slot_at(j, who):
        return jnp.clip(who - start_of(j), 0, window - 1)

    own_at = pl.multiple_of((i - start_of(i)) * cols, cols)
    own = pl.ds(own_at, cols)
    offsets = range(-(window - 1), window)

    def reads_me(dj):
        j = i + dj
        first = start_of(j)
        return (j >= 0) & (j < n_inst) & (i >= first) & (i < first + window)

    def read_by_me(dj):
        first = start_of(i)
        return (i + dj >= first) & (i + dj < first + window)

    def tell(condition, device):
        if condition is True:
            pl.semaphore_signal(barrier, inc=1, device_id=device, device_id_type=MESH)
        else:
            @pl.when(condition)
            def _():
                pl.semaphore_signal(barrier, inc=1, device_id=device, device_id_type=MESH)

    def one_if(condition):
        return jnp.where(condition, 1, 0)

    def sh_copy(dj, block, dc, way):
        j = i + dj
        slot = slot_at(j, i)
        at = pl.multiple_of(slot * cols, cols)
        return remote(
            shift_hbm, sh.at[2 * block:2 * block + 2, pl.ds(at, cols)],
            sh_send.at[dj + window - 1, way], sh_recv.at[slot, block], (j, c + dc),
        )

    def finish(packed, read):
        total = jnp.sum(packed, axis=1, keepdims=True)
        mu = [total[k:k + 1] for k in range(6)]
        at_x, at_r = coefficients(mu)
        for k in range(3):
            for row in range(2):
                b = [read(j, k, row) for j in range(4)]
                x_ref[k, row] = at_x[0] * b[0] + at_x[1] * b[1] + at_x[2] * b[2]
                r_ref[k, row] = at_r[0] * b[0] + at_r[1] * b[1] + at_r[2] * b[2] + at_r[3] * b[3]

    def moment_copy(d, core):
        to = lax.rem(m + d, n_pair)
        return remote(
            pack, gath.at[d], g_send.at[d, core], g_recv.at[d], (i, 2 * to + core)
        )

    def across_copy(d, core):
        to = lax.rem(i + d, n_inst)
        return remote(
            pack2, gath2.at[d], h_send.at[d, core], h_recv.at[d], (to, 2 * m + core)
        )

    def basis_copy(j):
        source = (u0, u1, u2, u3)[j]
        return remote(
            source.at[:, ROW_A:ROW_C, own], basis.at[j], b_send.at[j], b_recv.at[j], (i, c - 1)
        )

    def halo_copy(side, h):
        if side == 0:
            return remote(
                adj.at[:, :, 4, :, lanes(h)], adj.at[:, :, 0, :, lanes(h)],
                halo_send.at[h], halo_recv.at[0, h], (i, c + 2),
            )
        return remote(
            adj_hbm.at[:, :, 0, :, lanes(h)], adj.at[:, :, 5, :, lanes(h)],
            halo_send.at[h], halo_recv.at[1, h], (i, c - 1),
        )

    def give_copy(number):
        src, dst = (
            (adj_hbm, adj.at[:, :, 1:3]),
            (flux_hbm.at[:, :, :, 1], flux.at[:, :, :, 1]),
            (flux_hbm.at[:, :, :, 0], flux.at[:, :, :, 0]),
        )[number]
        return remote(src, dst, give_send.at[number], give_recv.at[number], (i, c + 1))

    @pl.when(c % 2 == 0)
    def even():
        if split:
            for d in range(n_inst):
                tell(True, (lax.rem(i + d, n_inst), c + 1))
        else:
            tell(True, (i, c + 1))
        expected = 0
        for dj in offsets:
            expected = expected + one_if(reads_me(dj)) + one_if(reads_me(dj) & has_prev)
        pl.semaphore_wait(barrier, expected)

        give_copy(0).start()
        for h in range(halves):
            @pl.when(has_prev)
            def _():
                halo_copy(1, h).start()
        give_copy(1).start()
        give_copy(2).start()
        for dj in offsets:
            @pl.when(reads_me(dj))
            def _():
                sh_copy(dj, 1, 1, 0).start()

            @pl.when(reads_me(dj) & has_prev)
            def _():
                sh_copy(dj, 3, -1, 1).start()

        for number in range(3):
            give_copy(number).wait_send()
        for h in range(halves):
            @pl.when(has_prev)
            def _():
                halo_copy(1, h).wait_send()
        for dj in offsets:
            @pl.when(reads_me(dj))
            def _():
                sh_copy(dj, 1, 1, 0).wait_send()

            @pl.when(reads_me(dj) & has_prev)
            def _():
                sh_copy(dj, 3, -1, 1).wait_send()

        for j in range(4):
            remote(basis.at[j], basis.at[j], b_send.at[j], b_recv.at[j], (i, c)).wait_recv()
        total = None
        if split:
            for d in range(n_inst):
                across_copy(d, 0).wait_recv()
                total = gath2[d] if total is None else total + gath2[d]
        else:
            for d in range(n_pair):
                moment_copy(d, 0).wait_recv()
                total = gath[d] if total is None else total + gath[d]
        finish(total, lambda j, k, row: basis[j, k, row])

    @pl.when(c % 2 == 1)
    def odd():
        loads = [
            pltpu.make_async_copy(adj_hbm, adj.at[:, :, 3:5], load_sem.at[0]),
            pltpu.make_async_copy(flux_hbm, flux.at[:, :, :, 2:4], load_sem.at[1]),
            pltpu.make_async_copy(shift_hbm, sh.at[4:6, own], load_sem.at[2]),
        ]
        for load in loads:
            load.start()

        for d in range(1, n_inst):
            tell(True, (lax.rem(i + d, n_inst), c))
        tell(has_next, (i, c + 2))
        for dj in offsets:
            ok = read_by_me(dj)
            tell(ok, (i + dj, c - 1))
            tell(ok & has_next, (i + dj, c + 1))
            tell(ok & has_prev, (i + dj, c - 2))
        expected = (n_inst - 1) + one_if(has_prev) + (n_inst if split else 1)
        for dj in offsets:
            expected = expected + one_if(reads_me(dj) & has_next)
        pl.semaphore_wait(barrier, expected)

        reaches = [r for r in (1, 2, 4, 8, 16, 32, 64) if r < n_pair]

        def inside(dm):
            return (m + dm >= 0) & (m + dm < n_pair)

        def hello(number):
            if number < len(reaches):
                for dm in (-reaches[number], reaches[number]):
                    @pl.when(inside(dm))
                    def _():
                        pl.semaphore_signal(
                            near.at[number], inc=1, device_id=(i, c + 2 * dm), device_id_type=MESH
                        )

        def heard(number):
            if number < len(reaches):
                count = 0
                for dm in (-reaches[number], reaches[number]):
                    count = count + one_if(inside(dm))
                pl.semaphore_wait(near.at[number], count)

        loads[0].wait()
        for h in range(halves):
            @pl.when(has_next)
            def _():
                halo_copy(0, h).start()
        hello(0)
        for dj in offsets:
            if dj != 0:
                @pl.when(reads_me(dj))
                def _():
                    sh_copy(dj, 2, 0, 0).start()

            @pl.when(reads_me(dj) & has_next)
            def _():
                sh_copy(dj, 0, 2, 1).start()

        @pl.when(jnp.logical_not(has_prev))
        def _():
            adj[:, :, 0] = jnp.zeros_like(adj[:, :, 0])
            sh[0:2] = jnp.zeros_like(sh[0:2])
            u0[:, 0:3] = jnp.zeros_like(u0[:, 0:3])

        @pl.when(jnp.logical_not(has_next))
        def _():
            adj[:, :, 5] = jnp.zeros_like(adj[:, :, 5])
            sh[6:8] = jnp.zeros_like(sh[6:8])
            u0[:, 7:10] = jnp.zeros_like(u0[:, 7:10])

        def y_copy(piece, d):
            j = lax.rem(i + d, n_inst)
            at = pl.multiple_of(start_of(j) * cols, cols)
            if piece < 2:
                row, ls = 2 - piece, slice(None)
            else:
                row, ls = (0, 3)[piece % 2], lanes(piece // 2 - 1)
            return remote(
                part.at[:, row, pl.ds(at, wy), ls], got.at[d - 1, :, row, :, ls],
                y_send.at[d - 1, piece], y_recv.at[d - 1, piece], (j, c),
            )

        chunks = [slice(y0, y0 + 16) for y0 in range(0, ny, 16)]

        def whole_terms(row):
            for ys in chunks:
                total = [None] * 3
                for v in range(nv):
                    a, b = v // n_v, v % n_v
                    step = adj[a, b, row + 2, ys].astype(F32) - adj[a, b, row, ys].astype(F32)
                    for k in range(3):
                        t = flux[a, b, k, row, ys].astype(F32) * step
                        total[k] = t if total[k] is None else total[k] + t
                for k in range(3):
                    part[k, row, ys] = total[k]

        def own_terms(row, beside, sign):
            for ys in chunks:
                total = [None] * 3
                for v in range(nv):
                    a, b = v // n_v, v % n_v
                    other = adj[a, b, beside, ys].astype(F32)
                    for k in range(3):
                        t = flux[a, b, k, row, ys].astype(F32) * other
                        total[k] = t if total[k] is None else total[k] + t
                for k in range(3):
                    part[k, row, ys] = total[k] if sign > 0 else -total[k]

        def halo_terms(row, beside, sign, h):
            ls = lanes(h)
            for ys in chunks:
                total = [part[k, row, ys, ls] for k in range(3)]
                for v in range(nv):
                    a, b = v // n_v, v % n_v
                    other = adj[a, b, beside, ys, ls].astype(F32)
                    for k in range(3):
                        t = flux[a, b, k, row, ys, ls].astype(F32) * other
                        total[k] = total[k] + t if sign > 0 else total[k] - t
                for k in range(3):
                    part[k, row, ys, ls] = total[k]

        loads[1].wait()
        give_copy(0).wait_recv()
        whole_terms(2)
        for d in range(1, n_inst):
            y_copy(0, d).start()
        own_terms(3, 3, -1)
        give_copy(1).wait_recv()
        whole_terms(1)
        for d in range(1, n_inst):
            y_copy(1, d).start()
        give_copy(2).wait_recv()
        own_terms(0, 2, 1)
        heard(0)
        hello(1)

        for h in range(halves):
            @pl.when(has_prev)
            def _():
                halo_copy(0, h).wait_recv()
            halo_terms(0, 0, -1, h)
            for d in range(1, n_inst):
                y_copy(2 + 2 * h, d).start()

            @pl.when(has_next)
            def _():
                halo_copy(1, h).wait_recv()
            halo_terms(3, 5, 1, h)
            for d in range(1, n_inst):
                y_copy(3 + 2 * h, d).start()
        heard(1)
        hello(2)

        my_at = pl.multiple_of(start_of(i) * cols, cols)

        def add_up(piece):
            for d in range(1, n_inst):
                y_copy(piece, d).wait_recv()
            if piece < 2:
                row, ls = 2 - piece, slice(None)
            else:
                row, ls = (0, 3)[piece % 2], lanes(piece // 2 - 1)
            for k in range(3):
                total = part[k, row, pl.ds(my_at, wy), ls]
                for d in range(1, n_inst):
                    total = total + got[d - 1, k, row, :, ls]
                u0[k, ROW_A + row, :, ls] = total

        inner_moves = (
            (5, 1, 1, has_next),
            (5, 9, -1, has_prev),
            (4, 8, -1, has_prev),
            (4, 0, 1, has_next),
        )

        def in_copy(number):
            src, dst, dm, _ = inner_moves[number]
            return remote(
                u0.at[:, src], u0.at[:, dst], in_send.at[number], in_recv.at[number], (i, c + 2 * dm)
            )

        def in_start(number):
            @pl.when(inner_moves[number][3])
            def _():
                in_copy(number).start()

        def in_wait(number):
            arrives = has_prev if inner_moves[number][2] == 1 else has_next

            @pl.when(arrives)
            def _():
                in_copy(number).wait_recv()

        def x_copy(side, h):
            src, dst, dm = ((ROW_A, 7, -1), (ROW_D, 2, 1))[side]
            return remote(
                u0.at[:, src, :, lanes(h)], u0.at[:, dst, :, lanes(h)],
                x_send.at[side, h], x_recv.at[side, h], (i, c + 2 * dm),
            )

        goes = (has_prev, has_next)

        add_up(0)
        in_start(0)
        in_start(1)
        add_up(1)
        in_start(2)
        for h in range(halves):
            for side in range(2):
                add_up(2 + 2 * h + side)

                @pl.when(goes[side])
                def _():
                    x_copy(side, h).start()
        in_start(3)

        for number in range(2, len(reaches)):
            heard(number)
            hello(number + 1)

        def sh_landed(slot, block):
            at = sh.at[2 * block:2 * block + 2, pl.ds(slot * cols, cols)]
            remote(at, at, sh_send.at[0, 0], sh_recv.at[slot, block], (i, c)).wait_recv()

        loads[2].wait()
        for slot in range(window):
            sh_landed(slot, 1)

            @pl.when(start_of(i) + slot != i)
            def _():
                sh_landed(slot, 2)

            @pl.when(has_prev)
            def _():
                sh_landed(slot, 0)

            @pl.when(has_next)
            def _():
                sh_landed(slot, 3)

        shape = (wy, nz)
        y_at = lax.broadcasted_iota(jnp.int32, shape, 0)
        z_at = lax.broadcasted_iota(jnp.int32, shape, 1)
        edges = (y_at == 0, y_at == wy - 1, z_at == 0, z_at == nz - 1)

        def valid_row(row):
            if row in PAIR_ROWS:
                return True
            return has_prev if row < ROW_A else has_next

        apply_operator(u0, u1, sh, (4, 5), valid_row, edges)
        for number in range(3):
            in_wait(number)
        for h in range(halves):
            for side in range(2):
                @pl.when(goes[1 - side])
                def _():
                    x_copy(side, h).wait_recv()

        apply_operator(u0, u1, sh, (2, 3), valid_row, edges)
        apply_operator(u0, u1, sh, (6, 7, 8), valid_row, edges)
        apply_operator(u1, u2, sh, (3, 4, 5, 6, 7), valid_row, edges)

        fields = (u0, u1, u2, u3)
        sums = []
        for n in range(6):
            total = energy(u2, sh, edges) if n == 5 else None
            a, b = fields[n // 2], fields[(n + 1) // 2]
            for k in range(3 if n < 5 else 0):
                for row in PAIR_ROWS:
                    term = a[k, row] * b[k, row]
                    total = term if total is None else total + term
            if split:
                total = jnp.where((y_at >= own_at) & (y_at < own_at + cols), total, 0.0)
            total = jnp.sum(total, axis=0, keepdims=True)
            sums.append(sum(total[:, z0:z0 + 128] for z0 in range(0, nz, 128)))
        sums.append(jnp.zeros((2, 128), F32))
        pack[...] = jnp.concatenate(sums, axis=0)
        cores = (1,) if split else (0, 1)
        for d in range(n_pair):
            for core in cores:
                if d > 0 or core == 0:
                    moment_copy(d, core).start()
        for j in range(3):
            basis_copy(j).start()
        in_wait(3)
        apply_operator(u0, u1, sh, (1,), valid_row, edges)
        apply_operator(u1, u2, sh, (2,), valid_row, edges)
        apply_operator(u2, u3, sh, PAIR_ROWS, valid_row, edges)
        basis_copy(3).start()

        total = pack[...]
        for d in range(1, n_pair):
            moment_copy(d, 1).wait_recv()
            total = total + gath[d]
        if split:
            pack2[...] = total
            for d in range(n_inst):
                for core in (0, 1):
                    if d > 0 or core == 0:
                        across_copy(d, core).start()
            for d in range(1, n_inst):
                across_copy(d, 1).wait_recv()
                total = total + gath2[d]
        finish(total, lambda j, k, row: fields[j][k, ROW_C + row, own])

        for j in range(4):
            basis_copy(j).wait_send()
        for d in range(n_pair):
            for core in cores:
                if d > 0 or core == 0:
                    moment_copy(d, core).wait_send()
        if split:
            for d in range(n_inst):
                for core in (0, 1):
                    if d > 0 or core == 0:
                        across_copy(d, core).wait_send()
        for number in range(4):
            @pl.when(inner_moves[number][3])
            def _():
                in_copy(number).wait_send()
        for h in range(halves):
            for side in range(2):
                @pl.when(goes[side])
                def _():
                    x_copy(side, h).wait_send()

            @pl.when(has_next)
            def _():
                halo_copy(0, h).wait_send()
        for piece in range(2 + 2 * halves):
            for d in range(1, n_inst):
                y_copy(piece, d).wait_send()
        for dj in offsets:
            if dj != 0:
                @pl.when(reads_me(dj))
                def _():
                    sh_copy(dj, 2, 0, 0).wait_send()

            @pl.when(reads_me(dj) & has_next)
            def _():
                sh_copy(dj, 0, 2, 1).wait_send()


def hand_over(x_in, r_in, x_out, r_out, sem):
    moves = [
        pltpu.make_async_copy(x_in, x_out, sem.at[0]),
        pltpu.make_async_copy(r_in, r_out, sem.at[1]),
    ]
    for move in moves:
        move.start()
    for move in moves:
        move.wait()


def local(n_inst, n_cell, adjoint, flux_jac, shift):
    rows, cols, nz = shift.shape
    n_i, n_v, _, ny, _ = adjoint.shape
    window = min(3, n_inst)
    wy = window * cols
    n_pair = n_cell // 2
    field = pltpu.VMEM((3, 2 * rows + 2 * HALO, wy, nz), F32)
    dma = pltpu.SemaphoreType.DMA
    out = jax.ShapeDtypeStruct((3, rows, cols, nz), F32)
    peers = max(n_inst - 1, 1)
    answers = pl.pallas_call(
        functools.partial(kernel, n_inst, n_cell, cols, window),
        out_shape=(out, out),
        in_specs=[pl.BlockSpec(memory_space=pltpu.HBM)] * 3,
        out_specs=(pl.BlockSpec(memory_space=pltpu.VMEM),) * 2,
        scratch_shapes=[
            pltpu.VMEM((n_i, n_v, 2 * rows + 2, ny, nz), adjoint.dtype),
            pltpu.VMEM((n_i, n_v, 3, 2 * rows, ny, nz), flux_jac.dtype),
            pltpu.VMEM((3, 2 * rows, ny, nz), F32),
            pltpu.VMEM((peers, 3, 2 * rows, wy, nz), F32),
            field, field, field, field,
            pltpu.VMEM((2 * rows + 4, wy, nz), F32),
            pltpu.VMEM((4, 3, rows, cols, nz), F32),
            pltpu.VMEM((8, 128), F32),
            pltpu.VMEM((n_pair, 8, 128), F32),
            pltpu.VMEM((8, 128), F32),
            pltpu.VMEM((n_inst, 8, 128), F32),
            dma((3,)),
            dma((3,)), dma((3,)),
            dma((2,)), dma((2, 2)),
            dma((2 * window - 1, 2)), dma((window, 4)),
            dma((peers, 6)), dma((peers, 6)),
            dma((4,)), dma((4,)),
            dma((2, 2)), dma((2, 2)),
            dma((4,)), dma((4,)),
            dma((n_pair, 2)), dma((n_pair,)),
            dma((n_inst, 2)), dma((n_inst,)),
            pltpu.SemaphoreType.REGULAR((7,)),
        ],
        compiler_params=pltpu.CompilerParams(
            collective_id=0, has_side_effects=True, vmem_limit_bytes=VMEM_GRANT
        ),
    )(*[pltpu.with_memory_space_constraint(a, pltpu.HBM) for a in (adjoint, flux_jac, shift)])
    return pl.pallas_call(
        hand_over,
        out_shape=(out, out),
        in_specs=[pl.BlockSpec(memory_space=pltpu.VMEM)] * 2,
        out_specs=(pl.BlockSpec(memory_space=pltpu.HBM),) * 2,
        scratch_shapes=[dma((2,))],
        compiler_params=pltpu.CompilerParams(vmem_limit_bytes=1 << 20),
    )(*answers)


def solution(mesh):
    placed = (
        P("inst", None, "cell", None, None),
        P("inst", None, None, "cell", None, None),
        P("cell", "inst", None),
    )
    return jax.shard_map(
        functools.partial(local, mesh.shape["inst"], mesh.shape["cell"]),
        mesh=mesh,
        in_specs=placed,
        out_specs=(P(None, "cell", "inst", None), P(None, "cell", "inst", None)),
        check_vma=False,
    )
```

```python
import functools

import jax
import jax.numpy as jnp
from jax import lax
from jax.experimental import pallas as pl
from jax.experimental.pallas import tpu as pltpu
from jax.sharding import PartitionSpec as P

ITERS = 3
LAME = 1.5
CENTER = 10.0
SPREAD = 8.0
HALO = 3
VMEM_GRANT = 40 << 20
MESH = pl.DeviceIdType.MESH
F32 = jnp.float32

ROW_A, ROW_B, ROW_C, ROW_D = 3, 4, 5, 6
PAIR_ROWS = (ROW_A, ROW_B, ROW_C, ROW_D)


def remote(src, dst, send_sem, recv_sem, device):
    return pltpu.make_async_remote_copy(
        src_ref=src,
        dst_ref=dst,
        send_sem=send_sem,
        recv_sem=recv_sem,
        device_id=device,
        device_id_type=MESH,
    )


def apply_operator(src, dst, sh, rows, valid_row, edges):
    y_first, y_last, z_first, z_last = edges
    wy, nz = src.shape[2], src.shape[3]

    def up_y(v):
        return jnp.where(y_last, 0.0, pltpu.roll(v, wy - 1, 0))

    def down_y(v):
        return jnp.where(y_first, 0.0, pltpu.roll(v, 1, 0))

    def up_z(v):
        return jnp.where(z_last, 0.0, pltpu.roll(v, nz - 1, 1))

    def down_z(v):
        return jnp.where(z_first, 0.0, pltpu.roll(v, 1, 1))

    def divergence(row):
        fields = [src[k, row] for k in range(3)]
        uy, uz = up_y(fields[1]), up_z(fields[2])
        dv = (src[0, row + 1] - fields[0]) + (uy - fields[1]) + (uz - fields[2])
        return fields, uy, uz, jnp.where(valid_row(row), dv, 0.0)

    before = {}
    for row in rows:
        if row - 1 not in before:
            before[row - 1] = divergence(row - 1)[3]
        fields, uy, uz, dv = divergence(row)
        before[row] = dv
        diag = sh[row - 1] + (6.0 - CENTER)
        shifted = [before[row - 1], down_y(dv), down_z(dv)]
        for k in range(3):
            u = fields[k]
            beside = src[k, row - 1] + src[k, row + 1]
            beside = beside + (uy if k == 1 else up_y(u)) + down_y(u)
            beside = beside + (uz if k == 2 else up_z(u)) + down_z(u)
            out = (diag * u - beside + LAME * (shifted[k] - dv)) * (1.0 / SPREAD)
            dst[k, row] = jnp.where(valid_row(row), out, 0.0)


def energy(src, sh, edges):
    _, y_last, _, z_last = edges
    wy, nz = src.shape[2], src.shape[3]
    total = None
    for row in PAIR_ROWS:
        dv = None
        for k in range(3):
            v = src[k, row]
            above = (
                src[k, row + 1],
                jnp.where(y_last, 0.0, pltpu.roll(v, wy - 1, 0)),
                jnp.where(z_last, 0.0, pltpu.roll(v, nz - 1, 1)),
            )
            step = above[k] - v
            dv = step if dv is None else dv + step
            diag = sh[row - 1] + (6.0 - CENTER)
            term = v * (diag * v - 2.0 * (above[0] + above[1] + above[2]))
            total = term if total is None else total + term
        total = total + LAME * (dv * dv)
    return total * (1.0 / SPREAD)


def coefficients(mu):
    def inner(a, b, skip=0):
        total = None
        for p, x in enumerate(a):
            for q, y in enumerate(b):
                if x is None or y is None:
                    continue
                term = x * y * mu[p + q]
                total = term if total is None else total + term
        return total

    def times(a):
        return [
            (CENTER * a[j] if j < len(a) else 0.0) + (SPREAD * a[j - 1] if j > 0 else 0.0)
            for j in range(len(a) + 1)
        ]

    one = jnp.ones_like(mu[0])
    solution_at, residual, direction = [], [one], [one]
    norm_now = mu[0]
    for sweep in range(ITERS):
        image = times(direction)
        alpha = norm_now / inner(direction, image)
        solution_at = [
            (solution_at[j] if j < len(solution_at) else 0.0) + alpha * direction[j]
            for j in range(len(direction))
        ]
        residual = [
            (residual[j] if j < len(residual) else 0.0) - alpha * image[j]
            for j in range(len(image))
        ]
        if sweep + 1 < ITERS:
            norm_next = inner(residual, residual)
            ratio = norm_next / norm_now
            direction = [
                residual[j] + (ratio * direction[j] if j < len(direction) else 0.0)
                for j in range(len(residual))
            ]
            norm_now = norm_next
    return solution_at, residual


def kernel(
    n_inst, n_cell, cols, window,
    adj_hbm, flux_hbm, shift_hbm, basis, sums,
    adj, flux, part, got, u0, u1, u2, u3, sh, pack, gath, pack2, gath2,
    load_sem, give_send, give_recv, halo_send, halo_recv, sh_send, sh_recv,
    y_send, y_recv, in_send, in_recv, x_send, x_recv, b_send, b_recv,
    g_send, g_recv, h_send, h_recv, near, shx_send, shx_recv,
):
    i, c = lax.axis_index("inst"), lax.axis_index("cell")
    n_pair = n_cell // 2
    m = c // 2
    wy = window * cols
    n_v = adj.shape[1]
    nv = adj.shape[0] * n_v
    ny, nz = adj.shape[3], adj.shape[4]
    halves = 2 if nz % 256 == 0 else 1
    split = window < n_inst
    has_prev, has_next = m > 0, m < n_pair - 1
    barrier = pltpu.get_barrier_semaphore()

    def lanes(h):
        return slice(h * (nz // halves), (h + 1) * (nz // halves))

    def start_of(j):
        return jnp.clip(j - 1, 0, n_inst - window)

    def slot_at(j, who):
        return jnp.clip(who - start_of(j), 0, window - 1)

    own_at = pl.multiple_of((i - start_of(i)) * cols, cols)
    own = pl.ds(own_at, cols)
    offsets = range(-(window - 1), window)

    def reads_me(dj):
        j = i + dj
        first = start_of(j)
        return (j >= 0) & (j < n_inst) & (i >= first) & (i < first + window)

    def read_by_me(dj):
        first = start_of(i)
        return (i + dj >= first) & (i + dj < first + window)

    def tell(condition, device):
        if condition is True:
            pl.semaphore_signal(barrier, inc=1, device_id=device, device_id_type=MESH)
        else:
            @pl.when(condition)
            def _():
                pl.semaphore_signal(barrier, inc=1, device_id=device, device_id_type=MESH)

    def one_if(condition):
        return jnp.where(condition, 1, 0)

    def sh_copy(dj, block, dc):
        j = i + dj
        slot = slot_at(j, i)
        at = pl.multiple_of(slot * cols, cols)
        return remote(
            shift_hbm, sh.at[2 * block:2 * block + 2, pl.ds(at, cols)],
            sh_send.at[dj + window - 1], sh_recv.at[slot, block], (j, c + dc),
        )

    def moment_copy(d, core):
        to = lax.rem(m + d, n_pair)
        return remote(
            pack, gath.at[d], g_send.at[d, core], g_recv.at[d], (i, 2 * to + core)
        )

    def across_copy(d, core):
        to = lax.rem(i + d, n_inst)
        return remote(
            pack2, gath2.at[d], h_send.at[d, core], h_recv.at[d], (to, 2 * m + core)
        )

    def basis_copy(j):
        source = (u0, u1, u2, u3)[j]
        return remote(
            source.at[:, ROW_A:ROW_C, own], basis.at[j], b_send.at[j], b_recv.at[j], (i, c - 1)
        )

    def halo_copy(side, h):
        if side == 0:
            return remote(
                adj.at[:, :, 4, :, lanes(h)], adj.at[:, :, 0, :, lanes(h)],
                halo_send.at[h], halo_recv.at[0, h], (i, c + 2),
            )
        return remote(
            adj_hbm.at[:, :, 0, :, lanes(h)], adj.at[:, :, 5, :, lanes(h)],
            halo_send.at[h], halo_recv.at[1, h], (i, c - 1),
        )

    def give_copy(number):
        src, dst = (
            (adj_hbm, adj.at[:, :, 1:3]),
            (flux_hbm.at[:, :, :, 1], flux.at[:, :, :, 1]),
            (flux_hbm.at[:, :, :, 0], flux.at[:, :, :, 0]),
        )[number]
        return remote(src, dst, give_send.at[number], give_recv.at[number], (i, c + 1))

    @pl.when(c % 2 == 0)
    def even():
        if split:
            for d in range(n_inst):
                tell(True, (lax.rem(i + d, n_inst), c + 1))
        else:
            tell(True, (i, c + 1))
        expected = one_if(has_prev)
        for dj in offsets:
            expected = expected + one_if(reads_me(dj))
        pl.semaphore_wait(barrier, expected)

        for h in range(halves):
            @pl.when(has_prev)
            def _():
                halo_copy(1, h).start()
        for number in range(3):
            give_copy(number).start()
        for dj in offsets:
            @pl.when(reads_me(dj))
            def _():
                sh_copy(dj, 1, 1).start()

        for number in range(3):
            give_copy(number).wait_send()
        for h in range(halves):
            @pl.when(has_prev)
            def _():
                halo_copy(1, h).wait_send()
        for dj in offsets:
            @pl.when(reads_me(dj))
            def _():
                sh_copy(dj, 1, 1).wait_send()

        for j in range(4):
            remote(basis.at[j], basis.at[j], b_send.at[j], b_recv.at[j], (i, c)).wait_recv()
        total = None
        if split:
            for d in range(n_inst):
                across_copy(d, 0).wait_recv()
                total = gath2[d] if total is None else total + gath2[d]
        else:
            for d in range(n_pair):
                moment_copy(d, 0).wait_recv()
                total = gath[d] if total is None else total + gath[d]
        sums[...] = total

    @pl.when(c % 2 == 1)
    def odd():
        loads = [
            pltpu.make_async_copy(adj_hbm, adj.at[:, :, 3:5], load_sem.at[0]),
            pltpu.make_async_copy(flux_hbm, flux.at[:, :, :, 2:4], load_sem.at[1]),
            pltpu.make_async_copy(shift_hbm, sh.at[4:6, own], load_sem.at[2]),
        ]
        for load in loads:
            load.start()

        for d in range(1, n_inst):
            tell(True, (lax.rem(i + d, n_inst), c))
        tell(has_prev, (i, c - 2))
        tell(has_next, (i, c + 2))
        tell(has_next, (i, c + 1))
        for dj in offsets:
            tell(read_by_me(dj), (i + dj, c - 1))
        expected = (n_inst - 1) + one_if(has_prev) + one_if(has_next) + (n_inst if split else 1)
        pl.semaphore_wait(barrier, expected)

        reaches = [r for r in (1, 2, 4, 8, 16, 32, 64) if r < n_pair]

        def inside(dm):
            return (m + dm >= 0) & (m + dm < n_pair)

        def hello(number):
            if number < len(reaches):
                for dm in (-reaches[number], reaches[number]):
                    @pl.when(inside(dm))
                    def _():
                        pl.semaphore_signal(
                            near.at[number], inc=1, device_id=(i, c + 2 * dm), device_id_type=MESH
                        )

        def heard(number):
            if number < len(reaches):
                count = 0
                for dm in (-reaches[number], reaches[number]):
                    count = count + one_if(inside(dm))
                pl.semaphore_wait(near.at[number], count)

        loads[0].wait()
        for h in range(halves):
            @pl.when(has_next)
            def _():
                halo_copy(0, h).start()
        hello(0)
        for dj in offsets:
            if dj != 0:
                @pl.when(reads_me(dj))
                def _():
                    sh_copy(dj, 2, 0).start()

        @pl.when(jnp.logical_not(has_prev))
        def _():
            adj[:, :, 0] = jnp.zeros_like(adj[:, :, 0])
            sh[0:2] = jnp.zeros_like(sh[0:2])
            u0[:, 0:3] = jnp.zeros_like(u0[:, 0:3])

        @pl.when(jnp.logical_not(has_next))
        def _():
            adj[:, :, 5] = jnp.zeros_like(adj[:, :, 5])
            sh[6:8] = jnp.zeros_like(sh[6:8])
            u0[:, 7:10] = jnp.zeros_like(u0[:, 7:10])

        def y_copy(piece, d):
            j = lax.rem(i + d, n_inst)
            at = pl.multiple_of(start_of(j) * cols, cols)
            if piece < 2:
                row, ls = 2 - piece, slice(None)
            else:
                row, ls = (0, 3)[piece % 2], lanes(piece // 2 - 1)
            return remote(
                part.at[:, row, pl.ds(at, wy), ls], got.at[d - 1, :, row, :, ls],
                y_send.at[d - 1, piece], y_recv.at[d - 1, piece], (j, c),
            )

        chunks = [slice(y0, y0 + 16) for y0 in range(0, ny, 16)]

        def whole_terms(row):
            for ys in chunks:
                total = [None] * 3
                for v in range(nv):
                    a, b = v // n_v, v % n_v
                    step = adj[a, b, row + 2, ys].astype(F32) - adj[a, b, row, ys].astype(F32)
                    for k in range(3):
                        t = flux[a, b, k, row, ys].astype(F32) * step
                        total[k] = t if total[k] is None else total[k] + t
                for k in range(3):
                    part[k, row, ys] = total[k]

        def own_terms(row, beside, sign):
            for ys in chunks:
                total = [None] * 3
                for v in range(nv):
                    a, b = v // n_v, v % n_v
                    other = adj[a, b, beside, ys].astype(F32)
                    for k in range(3):
                        t = flux[a, b, k, row, ys].astype(F32) * other
                        total[k] = t if total[k] is None else total[k] + t
                for k in range(3):
                    part[k, row, ys] = total[k] if sign > 0 else -total[k]

        def halo_terms(row, beside, sign, h):
            ls = lanes(h)
            for ys in chunks:
                total = [part[k, row, ys, ls] for k in range(3)]
                for v in range(nv):
                    a, b = v // n_v, v % n_v
                    other = adj[a, b, beside, ys, ls].astype(F32)
                    for k in range(3):
                        t = flux[a, b, k, row, ys, ls].astype(F32) * other
                        total[k] = total[k] + t if sign > 0 else total[k] - t
                for k in range(3):
                    part[k, row, ys, ls] = total[k]

        goes = (has_prev, has_next)

        def sh_rows_copy(side):
            src, dst = ((2, 6), (4, 0))[side]
            return remote(
                sh.at[src:src + 2], sh.at[dst:dst + 2],
                shx_send.at[side], shx_recv.at[side], (i, c + 2 * (2 * side - 1)),
            )

        def sh_landed(slot, block):
            at = sh.at[2 * block:2 * block + 2, pl.ds(slot * cols, cols)]
            remote(at, at, sh_send.at[0], sh_recv.at[slot, block], (i, c)).wait_recv()

        def shift_rows():
            loads[2].wait()
            for slot in range(window):
                sh_landed(slot, 1)

                @pl.when(start_of(i) + slot != i)
                def _():
                    sh_landed(slot, 2)
            for side in range(2):
                @pl.when(goes[side])
                def _():
                    sh_rows_copy(side).start()

        loads[1].wait()
        give_copy(0).wait_recv()
        whole_terms(2)
        for d in range(1, n_inst):
            y_copy(0, d).start()
        own_terms(3, 3, -1)
        give_copy(1).wait_recv()
        whole_terms(1)
        for d in range(1, n_inst):
            y_copy(1, d).start()
        give_copy(2).wait_recv()
        own_terms(0, 2, 1)
        heard(0)
        hello(1)

        for h in range(halves):
            @pl.when(has_prev)
            def _():
                halo_copy(0, h).wait_recv()
            halo_terms(0, 0, -1, h)
            for d in range(1, n_inst):
                y_copy(2 + 2 * h, d).start()

            @pl.when(has_next)
            def _():
                halo_copy(1, h).wait_recv()
            halo_terms(3, 5, 1, h)
            for d in range(1, n_inst):
                y_copy(3 + 2 * h, d).start()
            if h == 0:
                shift_rows()
        heard(1)
        hello(2)

        my_at = pl.multiple_of(start_of(i) * cols, cols)

        def add_up(piece):
            for d in range(1, n_inst):
                y_copy(piece, d).wait_recv()
            if piece < 2:
                row, ls = 2 - piece, slice(None)
            else:
                row, ls = (0, 3)[piece % 2], lanes(piece // 2 - 1)
            for k in range(3):
                total = part[k, row, pl.ds(my_at, wy), ls]
                for d in range(1, n_inst):
                    total = total + got[d - 1, k, row, :, ls]
                u0[k, ROW_A + row, :, ls] = total

        inner_moves = (
            (5, 1, 1, has_next),
            (5, 9, -1, has_prev),
            (4, 8, -1, has_prev),
            (4, 0, 1, has_next),
        )

        def in_copy(number):
            src, dst, dm, _ = inner_moves[number]
            return remote(
                u0.at[:, src], u0.at[:, dst], in_send.at[number], in_recv.at[number], (i, c + 2 * dm)
            )

        def in_start(number):
            @pl.when(inner_moves[number][3])
            def _():
                in_copy(number).start()

        def in_wait(number):
            arrives = has_prev if inner_moves[number][2] == 1 else has_next

            @pl.when(arrives)
            def _():
                in_copy(number).wait_recv()

        def x_copy(side, h):
            src, dst, dm = ((ROW_A, 7, -1), (ROW_D, 2, 1))[side]
            return remote(
                u0.at[:, src, :, lanes(h)], u0.at[:, dst, :, lanes(h)],
                x_send.at[side, h], x_recv.at[side, h], (i, c + 2 * dm),
            )

        add_up(0)
        in_start(0)
        in_start(1)
        add_up(1)
        in_start(2)
        for h in range(halves):
            for side in range(2):
                add_up(2 + 2 * h + side)

                @pl.when(goes[side])
                def _():
                    x_copy(side, h).start()
        in_start(3)

        for number in range(2, len(reaches)):
            heard(number)
            hello(number + 1)

        shape = (wy, nz)
        y_at = lax.broadcasted_iota(jnp.int32, shape, 0)
        z_at = lax.broadcasted_iota(jnp.int32, shape, 1)
        edges = (y_at == 0, y_at == wy - 1, z_at == 0, z_at == nz - 1)

        def valid_row(row):
            if row in PAIR_ROWS:
                return True
            return has_prev if row < ROW_A else has_next

        fields = (u0, u1, u2, u3)
        lane = lax.broadcasted_iota(jnp.int32, (1, 128), 1)

        def moment(n):
            total = energy(u2, sh, edges) if n == 5 else None
            a, b = fields[n // 2], fields[(n + 1) // 2]
            for k in range(3 if n < 5 else 0):
                for row in PAIR_ROWS:
                    term = a[k, row] * b[k, row]
                    total = term if total is None else total + term
            if split:
                total = jnp.where((y_at >= own_at) & (y_at < own_at + cols), total, 0.0)
            value = jnp.sum(jnp.sum(total, axis=0, keepdims=True), axis=1, keepdims=True)
            return jnp.where(lane == n, value, 0.0)

        def arrived(side):
            there = goes[side]
            in_wait(0) if side == 0 else (in_wait(1), in_wait(2))

            @pl.when(there)
            def _():
                sh_rows_copy(1 - side).wait_recv()
                for h in range(halves):
                    x_copy(1 - side, h).wait_recv()

        apply_operator(u0, u1, sh, (4, 5), valid_row, edges)
        pack[...] = moment(0)
        arrived(1)
        apply_operator(u0, u1, sh, (6, 7, 8), valid_row, edges)
        apply_operator(u1, u2, sh, (6, 7), valid_row, edges)
        arrived(0)
        apply_operator(u0, u1, sh, (2, 3), valid_row, edges)
        apply_operator(u1, u2, sh, (3, 4, 5), valid_row, edges)

        pack[...] += moment(1) + moment(2) + moment(3) + moment(4) + moment(5)
        cores = (1,) if split else (0, 1)
        for d in range(n_pair):
            for core in cores:
                if d > 0 or core == 0:
                    moment_copy(d, core).start()
        for j in range(3):
            basis_copy(j).start()
        in_wait(3)
        apply_operator(u0, u1, sh, (1,), valid_row, edges)
        apply_operator(u1, u2, sh, (2,), valid_row, edges)
        apply_operator(u2, u3, sh, PAIR_ROWS, valid_row, edges)
        basis_copy(3).start()

        for j in range(4):
            basis[j] = fields[j][:, ROW_C:ROW_C + 2, own]
        total = pack[...]
        for d in range(1, n_pair):
            moment_copy(d, 1).wait_recv()
            total = total + gath[d]
        if split:
            pack2[...] = total
            for d in range(n_inst):
                for core in (0, 1):
                    if d > 0 or core == 0:
                        across_copy(d, core).start()
            for d in range(1, n_inst):
                across_copy(d, 1).wait_recv()
                total = total + gath2[d]
        sums[...] = total

        for j in range(4):
            basis_copy(j).wait_send()
        for d in range(n_pair):
            for core in cores:
                if d > 0 or core == 0:
                    moment_copy(d, core).wait_send()
        if split:
            for d in range(n_inst):
                for core in (0, 1):
                    if d > 0 or core == 0:
                        across_copy(d, core).wait_send()
        for number in range(4):
            @pl.when(inner_moves[number][3])
            def _():
                in_copy(number).wait_send()
        for h in range(halves):
            for side in range(2):
                @pl.when(goes[side])
                def _():
                    x_copy(side, h).wait_send()

            @pl.when(has_next)
            def _():
                halo_copy(0, h).wait_send()
        for piece in range(2 + 2 * halves):
            for d in range(1, n_inst):
                y_copy(piece, d).wait_send()
        for dj in offsets:
            if dj != 0:
                @pl.when(reads_me(dj))
                def _():
                    sh_copy(dj, 2, 0).wait_send()
        for side in range(2):
            @pl.when(goes[side])
            def _():
                sh_rows_copy(side).wait_send()


def combine(basis, sums, x_out, r_out, x, r, sem):
    lane = lax.broadcasted_iota(jnp.int32, sums.shape, 1)
    mu = [
        jnp.sum(jnp.where(lane == m, sums[...], 0.0), axis=1, keepdims=True) for m in range(6)
    ]
    at_x, at_r = coefficients(mu)
    moves = []
    for k in range(3):
        b = [basis[j, k] for j in range(4)]
        x[k] = at_x[0] * b[0] + at_x[1] * b[1] + at_x[2] * b[2]
        r[k] = at_r[0] * b[0] + at_r[1] * b[1] + at_r[2] * b[2] + at_r[3] * b[3]
        for q, (src, dst) in enumerate(((x, x_out), (r, r_out))):
            moves.append(pltpu.make_async_copy(src.at[k], dst.at[k], sem.at[q, k]))
            moves[-1].start()
    for move in moves:
        move.wait()


def local(n_inst, n_cell, adjoint, flux_jac, shift):
    rows, cols, nz = shift.shape
    n_i, n_v, _, ny, _ = adjoint.shape
    window = min(3, n_inst)
    wy = window * cols
    n_pair = n_cell // 2
    field = pltpu.VMEM((3, 2 * rows + 2 * HALO, wy, nz), F32)
    dma = pltpu.SemaphoreType.DMA
    out = jax.ShapeDtypeStruct((3, rows, cols, nz), F32)
    peers = max(n_inst - 1, 1)
    answers = pl.pallas_call(
        functools.partial(kernel, n_inst, n_cell, cols, window),
        out_shape=(
            jax.ShapeDtypeStruct((4, 3, rows, cols, nz), F32),
            jax.ShapeDtypeStruct((1, 128), F32),
        ),
        in_specs=[pl.BlockSpec(memory_space=pltpu.HBM)] * 3,
        out_specs=(pl.BlockSpec(memory_space=pltpu.VMEM),) * 2,
        scratch_shapes=[
            pltpu.VMEM((n_i, n_v, 2 * rows + 2, ny, nz), adjoint.dtype),
            pltpu.VMEM((n_i, n_v, 3, 2 * rows, ny, nz), flux_jac.dtype),
            pltpu.VMEM((3, 2 * rows, ny, nz), F32),
            pltpu.VMEM((peers, 3, 2 * rows, wy, nz), F32),
            field, field, field, field,
            pltpu.VMEM((2 * rows + 4, wy, nz), F32),
            pltpu.VMEM((1, 128), F32),
            pltpu.VMEM((n_pair, 1, 128), F32),
            pltpu.VMEM((1, 128), F32),
            pltpu.VMEM((n_inst, 1, 128), F32),
            dma((3,)),
            dma((3,)), dma((3,)),
            dma((2,)), dma((2, 2)),
            dma((2 * window - 1,)), dma((window, 3)),
            dma((peers, 6)), dma((peers, 6)),
            dma((4,)), dma((4,)),
            dma((2, 2)), dma((2, 2)),
            dma((4,)), dma((4,)),
            dma((n_pair, 2)), dma((n_pair,)),
            dma((n_inst, 2)), dma((n_inst,)),
            pltpu.SemaphoreType.REGULAR((7,)),
            dma((2,)), dma((2,)),
        ],
        compiler_params=pltpu.CompilerParams(
            collective_id=0, has_side_effects=True, vmem_limit_bytes=VMEM_GRANT
        ),
    )(*[pltpu.with_memory_space_constraint(a, pltpu.HBM) for a in (adjoint, flux_jac, shift)])
    return pl.pallas_call(
        combine,
        out_shape=(out, out),
        in_specs=[pl.BlockSpec(memory_space=pltpu.VMEM)] * 2,
        out_specs=(pl.BlockSpec(memory_space=pltpu.HBM),) * 2,
        scratch_shapes=[
            pltpu.VMEM((3, rows, cols, nz), F32), pltpu.VMEM((3, rows, cols, nz), F32), dma((2, 3)),
        ],
        compiler_params=pltpu.CompilerParams(vmem_limit_bytes=2 << 20),
    )(*answers)


def solution(mesh):
    placed = (
        P("inst", None, "cell", None, None),
        P("inst", None, None, "cell", None, None),
        P("cell", "inst", None),
    )
    return jax.shard_map(
        functools.partial(local, mesh.shape["inst"], mesh.shape["cell"]),
        mesh=mesh,
        in_specs=placed,
        out_specs=(P(None, "cell", "inst", None), P(None, "cell", "inst", None)),
        check_vma=False,
    )
```

```python
import functools

import jax
import jax.numpy as jnp
from jax import lax
from jax.experimental import pallas as pl
from jax.experimental.pallas import tpu as pltpu
from jax.sharding import PartitionSpec as P

ITERS = 3
LAME = 1.5
CENTER = 10.0
SPREAD = 8.0
HALO = 3
VMEM_GRANT = 40 << 20
MESH = pl.DeviceIdType.MESH
F32 = jnp.float32

ROW_A, ROW_B, ROW_C, ROW_D = 3, 4, 5, 6
PAIR_ROWS = (ROW_A, ROW_B, ROW_C, ROW_D)


def remote(src, dst, send_sem, recv_sem, device):
    return pltpu.make_async_remote_copy(
        src_ref=src,
        dst_ref=dst,
        send_sem=send_sem,
        recv_sem=recv_sem,
        device_id=device,
        device_id_type=MESH,
    )


def beside_of(v, axis, step, unit):
    n = v.shape[axis]
    if n % unit:
        unit = n
    at = lax.broadcasted_iota(jnp.int32, v.shape[:axis] + (unit,) + v.shape[axis + 1:], axis)
    seam = at == (unit - 1 if step == 1 else 0)
    tiles = [lax.slice_in_dim(v, p, p + unit, axis=axis) for p in range(0, n, unit)]
    turned = [pltpu.roll(t, unit - 1 if step == 1 else 1, axis) for t in tiles]
    outs = []
    for p in range(len(tiles)):
        beyond = p + step
        inside = 0 <= beyond < len(tiles)
        outs.append(jnp.where(seam, turned[beyond] if inside else 0.0, turned[p]))
    return jnp.concatenate(outs, axis=axis)


def apply_operator(src, dst, sh, rows, valid_row):
    up_y = functools.partial(beside_of, axis=0, step=1, unit=8)
    down_y = functools.partial(beside_of, axis=0, step=-1, unit=8)
    up_z = functools.partial(beside_of, axis=1, step=1, unit=128)
    down_z = functools.partial(beside_of, axis=1, step=-1, unit=128)

    def divergence(row):
        fields = [src[k, row] for k in range(3)]
        uy, uz = up_y(fields[1]), up_z(fields[2])
        dv = (src[0, row + 1] - fields[0]) + (uy - fields[1]) + (uz - fields[2])
        return fields, uy, uz, jnp.where(valid_row(row), dv, 0.0)

    before = {}
    for row in rows:
        if row - 1 not in before:
            before[row - 1] = divergence(row - 1)[3]
        fields, uy, uz, dv = divergence(row)
        before[row] = dv
        diag = sh[row - 1] + (6.0 - CENTER)
        shifted = [before[row - 1], down_y(dv), down_z(dv)]
        for k in range(3):
            u = fields[k]
            beside = src[k, row - 1] + src[k, row + 1]
            beside = beside + (uy if k == 1 else up_y(u)) + down_y(u)
            beside = beside + (uz if k == 2 else up_z(u)) + down_z(u)
            out = (diag * u - beside + LAME * (shifted[k] - dv)) * (1.0 / SPREAD)
            dst[k, row] = jnp.where(valid_row(row), out, 0.0)


def energy(src, sh):
    total = None
    for row in PAIR_ROWS:
        dv = None
        for k in range(3):
            v = src[k, row]
            above = (
                src[k, row + 1],
                beside_of(v, 0, 1, 8),
                beside_of(v, 1, 1, 128),
            )
            step = above[k] - v
            dv = step if dv is None else dv + step
            diag = sh[row - 1] + (6.0 - CENTER)
            term = v * (diag * v - 2.0 * (above[0] + above[1] + above[2]))
            total = term if total is None else total + term
        total = total + LAME * (dv * dv)
    return total * (1.0 / SPREAD)


def coefficients(mu):
    def inner(a, b, skip=0):
        total = None
        for p, x in enumerate(a):
            for q, y in enumerate(b):
                if x is None or y is None:
                    continue
                term = x * y * mu[p + q]
                total = term if total is None else total + term
        return total

    def times(a):
        return [
            (CENTER * a[j] if j < len(a) else 0.0) + (SPREAD * a[j - 1] if j > 0 else 0.0)
            for j in range(len(a) + 1)
        ]

    one = jnp.ones_like(mu[0])
    solution_at, residual, direction = [], [one], [one]
    norm_now = mu[0]
    for sweep in range(ITERS):
        image = times(direction)
        alpha = norm_now / inner(direction, image)
        solution_at = [
            (solution_at[j] if j < len(solution_at) else 0.0) + alpha * direction[j]
            for j in range(len(direction))
        ]
        residual = [
            (residual[j] if j < len(residual) else 0.0) - alpha * image[j]
            for j in range(len(image))
        ]
        if sweep + 1 < ITERS:
            norm_next = inner(residual, residual)
            ratio = norm_next / norm_now
            direction = [
                residual[j] + (ratio * direction[j] if j < len(direction) else 0.0)
                for j in range(len(residual))
            ]
            norm_now = norm_next
    return solution_at, residual


def kernel(
    n_inst, n_cell, cols, window,
    adj_hbm, flux_hbm, shift_hbm, basis, sums,
    adj, flux, part, got, u0, u1, u2, u3, sh, pack, gath, pack2, gath2,
    load_sem, give_send, give_recv, halo_send, halo_recv, sh_send, sh_recv,
    y_send, y_recv, in_send, in_recv, x_send, x_recv, b_send, b_recv,
    g_send, g_recv, h_send, h_recv, near, shx_send, shx_recv,
):
    i, c = lax.axis_index("inst"), lax.axis_index("cell")
    n_pair = n_cell // 2
    m = c // 2
    wy = window * cols
    n_v = adj.shape[1]
    nv = adj.shape[0] * n_v
    ny, nz = adj.shape[3], adj.shape[4]
    halves = 2 if nz % 256 == 0 else 1
    split = window < n_inst
    has_prev, has_next = m > 0, m < n_pair - 1
    barrier = pltpu.get_barrier_semaphore()

    def lanes(h):
        return slice(h * (nz // halves), (h + 1) * (nz // halves))

    def start_of(j):
        return jnp.clip(j - 1, 0, n_inst - window)

    def slot_at(j, who):
        return jnp.clip(who - start_of(j), 0, window - 1)

    own_at = pl.multiple_of((i - start_of(i)) * cols, cols)
    own = pl.ds(own_at, cols)
    offsets = range(-(window - 1), window)

    def reads_me(dj):
        j = i + dj
        first = start_of(j)
        return (j >= 0) & (j < n_inst) & (i >= first) & (i < first + window)

    def read_by_me(dj):
        first = start_of(i)
        return (i + dj >= first) & (i + dj < first + window)

    def tell(condition, device):
        if condition is True:
            pl.semaphore_signal(barrier, inc=1, device_id=device, device_id_type=MESH)
        else:
            @pl.when(condition)
            def _():
                pl.semaphore_signal(barrier, inc=1, device_id=device, device_id_type=MESH)

    def one_if(condition):
        return jnp.where(condition, 1, 0)

    def sh_copy(dj, block, dc):
        j = i + dj
        slot = slot_at(j, i)
        at = pl.multiple_of(slot * cols, cols)
        return remote(
            shift_hbm, sh.at[2 * block:2 * block + 2, pl.ds(at, cols)],
            sh_send.at[dj + window - 1], sh_recv.at[slot, block], (j, c + dc),
        )

    def moment_copy(to, core):
        return remote(
            pack, gath.at[m], g_send.at[to, core], g_recv.at[m], (i, 2 * to + core)
        )

    def moment_from(pair):
        return remote(pack, gath.at[pair], g_send.at[0, 0], g_recv.at[pair], (i, c))

    def across_copy(d, core):
        to = lax.rem(i + d, n_inst)
        return remote(
            pack2, gath2.at[d], h_send.at[d, core], h_recv.at[d], (to, 2 * m + core)
        )

    def basis_copy(j):
        source = (u0, u1, u2, u3)[j]
        return remote(
            source.at[:, ROW_A:ROW_C, own], basis.at[j], b_send.at[j], b_recv.at[j], (i, c - 1)
        )

    def halo_copy(side, h):
        if side == 0:
            return remote(
                adj.at[:, :, 4, :, lanes(h)], adj.at[:, :, 0, :, lanes(h)],
                halo_send.at[h], halo_recv.at[0, h], (i, c + 2),
            )
        return remote(
            adj_hbm.at[:, :, 0, :, lanes(h)], adj.at[:, :, 5, :, lanes(h)],
            halo_send.at[h], halo_recv.at[1, h], (i, c - 1),
        )

    def give_copy(number):
        src, dst = (
            (adj_hbm, adj.at[:, :, 1:3]),
            (flux_hbm.at[:, :, :, 1], flux.at[:, :, :, 1]),
            (flux_hbm.at[:, :, :, 0], flux.at[:, :, :, 0]),
        )[number]
        return remote(src, dst, give_send.at[number], give_recv.at[number], (i, c + 1))

    @pl.when(c % 2 == 0)
    def even():
        if split:
            for d in range(n_inst):
                tell(True, (lax.rem(i + d, n_inst), c + 1))
        else:
            tell(True, (i, c + 1))
        expected = one_if(has_prev)
        for dj in offsets:
            expected = expected + one_if(reads_me(dj))
        pl.semaphore_wait(barrier, expected)

        for h in range(halves):
            @pl.when(has_prev)
            def _():
                halo_copy(1, h).start()
        for number in range(3):
            give_copy(number).start()
        for dj in offsets:
            @pl.when(reads_me(dj))
            def _():
                sh_copy(dj, 1, 1).start()

        for number in range(3):
            give_copy(number).wait_send()
        for h in range(halves):
            @pl.when(has_prev)
            def _():
                halo_copy(1, h).wait_send()
        for dj in offsets:
            @pl.when(reads_me(dj))
            def _():
                sh_copy(dj, 1, 1).wait_send()

        for j in range(4):
            remote(basis.at[j], basis.at[j], b_send.at[j], b_recv.at[j], (i, c)).wait_recv()
        total = None
        if split:
            for d in range(n_inst):
                across_copy(d, 0).wait_recv()
                total = gath2[d] if total is None else total + gath2[d]
        else:
            for d in range(n_pair):
                moment_from(d).wait_recv()
                total = gath[d] if total is None else total + gath[d]
        sums[...] = total

    @pl.when(c % 2 == 1)
    def odd():
        tell(has_prev, (i, c - 2))
        tell(has_next, (i, c + 1))
        tell(has_next, (i, c + 2))
        for dj in offsets:
            tell(read_by_me(dj), (i + dj, c - 1))
        for d in range(1, n_inst):
            tell(True, (lax.rem(i + d, n_inst), c))
        loads = [
            pltpu.make_async_copy(adj_hbm, adj.at[:, :, 3:5], load_sem.at[0]),
            pltpu.make_async_copy(flux_hbm, flux.at[:, :, :, 2:4], load_sem.at[1]),
            pltpu.make_async_copy(shift_hbm, sh.at[4:6, own], load_sem.at[2]),
        ]
        for load in loads:
            load.start()
        expected = (n_inst - 1) + one_if(has_prev) + one_if(has_next) + (n_inst if split else 1)
        pl.semaphore_wait(barrier, expected)

        reaches = [r for r in (1, 2, 4, 8, 16, 32, 64) if r < n_pair]

        def inside(dm):
            return (m + dm >= 0) & (m + dm < n_pair)

        def hello(number):
            if number < len(reaches):
                for dm in (-reaches[number], reaches[number]):
                    @pl.when(inside(dm))
                    def _():
                        pl.semaphore_signal(
                            near.at[number], inc=1, device_id=(i, c + 2 * dm), device_id_type=MESH
                        )

        def heard(number):
            if number < len(reaches):
                count = 0
                for dm in (-reaches[number], reaches[number]):
                    count = count + one_if(inside(dm))
                pl.semaphore_wait(near.at[number], count)

        loads[0].wait()
        for h in range(halves):
            @pl.when(has_next)
            def _():
                halo_copy(0, h).start()
        hello(0)
        for dj in offsets:
            if dj != 0:
                @pl.when(reads_me(dj))
                def _():
                    sh_copy(dj, 2, 0).start()

        @pl.when(jnp.logical_not(has_prev))
        def _():
            adj[:, :, 0] = jnp.zeros_like(adj[:, :, 0])
            sh[0:2] = jnp.zeros_like(sh[0:2])
            u0[:, 0:3] = jnp.zeros_like(u0[:, 0:3])

        @pl.when(jnp.logical_not(has_next))
        def _():
            adj[:, :, 5] = jnp.zeros_like(adj[:, :, 5])
            sh[6:8] = jnp.zeros_like(sh[6:8])
            u0[:, 7:10] = jnp.zeros_like(u0[:, 7:10])

        def y_copy(piece, d):
            j = lax.rem(i + d, n_inst)
            at = pl.multiple_of(start_of(j) * cols, cols)
            if piece < 2:
                row, ls = 2 - piece, slice(None)
            else:
                row, ls = (0, 3)[piece % 2], lanes(piece // 2 - 1)
            return remote(
                part.at[:, row, pl.ds(at, wy), ls], got.at[d - 1, :, row, :, ls],
                y_send.at[d - 1, piece], y_recv.at[d - 1, piece], (j, c),
            )

        chunks = [slice(y0, y0 + 16) for y0 in range(0, ny, 16)]

        def whole_terms(row):
            for ys in chunks:
                total = [None] * 3
                for v in range(nv):
                    a, b = v // n_v, v % n_v
                    step = adj[a, b, row + 2, ys].astype(F32) - adj[a, b, row, ys].astype(F32)
                    for k in range(3):
                        t = flux[a, b, k, row, ys].astype(F32) * step
                        total[k] = t if total[k] is None else total[k] + t
                for k in range(3):
                    part[k, row, ys] = total[k]

        def own_terms(row, beside, sign):
            for ys in chunks:
                total = [None] * 3
                for v in range(nv):
                    a, b = v // n_v, v % n_v
                    other = adj[a, b, beside, ys].astype(F32)
                    for k in range(3):
                        t = flux[a, b, k, row, ys].astype(F32) * other
                        total[k] = t if total[k] is None else total[k] + t
                for k in range(3):
                    part[k, row, ys] = total[k] if sign > 0 else -total[k]

        def halo_terms(row, beside, sign, h):
            ls = lanes(h)
            for ys in chunks:
                total = [part[k, row, ys, ls] for k in range(3)]
                for v in range(nv):
                    a, b = v // n_v, v % n_v
                    other = adj[a, b, beside, ys, ls].astype(F32)
                    for k in range(3):
                        t = flux[a, b, k, row, ys, ls].astype(F32) * other
                        total[k] = total[k] + t if sign > 0 else total[k] - t
                for k in range(3):
                    part[k, row, ys, ls] = total[k]

        goes = (has_prev, has_next)

        def sh_rows_copy(side):
            src, dst = ((2, 6), (4, 0))[side]
            return remote(
                sh.at[src:src + 2], sh.at[dst:dst + 2],
                shx_send.at[side], shx_recv.at[side], (i, c + 2 * (2 * side - 1)),
            )

        def sh_landed(slot, block):
            at = sh.at[2 * block:2 * block + 2, pl.ds(slot * cols, cols)]
            remote(at, at, sh_send.at[0], sh_recv.at[slot, block], (i, c)).wait_recv()

        def shift_rows():
            loads[2].wait()
            for slot in range(window):
                sh_landed(slot, 1)

                @pl.when(start_of(i) + slot != i)
                def _():
                    sh_landed(slot, 2)
            for side in range(2):
                @pl.when(goes[side])
                def _():
                    sh_rows_copy(side).start()

        loads[1].wait()
        give_copy(0).wait_recv()
        whole_terms(2)
        for d in range(1, n_inst):
            y_copy(0, d).start()
        own_terms(3, 3, -1)
        give_copy(1).wait_recv()
        whole_terms(1)
        for d in range(1, n_inst):
            y_copy(1, d).start()
        give_copy(2).wait_recv()
        own_terms(0, 2, 1)
        heard(0)
        hello(1)

        for h in range(halves):
            @pl.when(has_prev)
            def _():
                halo_copy(0, h).wait_recv()
            halo_terms(0, 0, -1, h)
            for d in range(1, n_inst):
                y_copy(2 + 2 * h, d).start()

            @pl.when(has_next)
            def _():
                halo_copy(1, h).wait_recv()
            halo_terms(3, 5, 1, h)
            for d in range(1, n_inst):
                y_copy(3 + 2 * h, d).start()
            if h == 0:
                shift_rows()

        my_at = pl.multiple_of(start_of(i) * cols, cols)

        def add_up(piece):
            for d in range(1, n_inst):
                y_copy(piece, d).wait_recv()
            if piece < 2:
                row, ls = 2 - piece, slice(None)
            else:
                row, ls = (0, 3)[piece % 2], lanes(piece // 2 - 1)
            for k in range(3):
                total = part[k, row, pl.ds(my_at, wy), ls]
                for d in range(1, n_inst):
                    total = total + got[d - 1, k, row, :, ls]
                u0[k, ROW_A + row, :, ls] = total

        inner_moves = (
            (5, 1, 1, has_next),
            (5, 9, -1, has_prev),
            (4, 8, -1, has_prev),
            (4, 0, 1, has_next),
        )

        def in_copy(number):
            src, dst, dm, _ = inner_moves[number]
            return remote(
                u0.at[:, src], u0.at[:, dst], in_send.at[number], in_recv.at[number], (i, c + 2 * dm)
            )

        def in_start(number):
            @pl.when(inner_moves[number][3])
            def _():
                in_copy(number).start()

        def in_wait(number):
            arrives = has_prev if inner_moves[number][2] == 1 else has_next

            @pl.when(arrives)
            def _():
                in_copy(number).wait_recv()

        def x_copy(side, h):
            src, dst, dm = ((ROW_A, 7, -1), (ROW_D, 2, 1))[side]
            return remote(
                u0.at[:, src, :, lanes(h)], u0.at[:, dst, :, lanes(h)],
                x_send.at[side, h], x_recv.at[side, h], (i, c + 2 * dm),
            )

        add_up(0)
        in_start(0)
        in_start(1)
        add_up(1)
        in_start(2)
        for h in range(halves):
            for side in range(2):
                add_up(2 + 2 * h + side)

                @pl.when(goes[side])
                def _():
                    x_copy(side, h).start()

        heard(1)
        hello(2)

        shape = (wy, nz)
        y_at = lax.broadcasted_iota(jnp.int32, shape, 0)

        def valid_row(row):
            if row in PAIR_ROWS:
                return True
            return has_prev if row < ROW_A else has_next

        fields = (u0, u1, u2, u3)
        lane = lax.broadcasted_iota(jnp.int32, (1, 128), 1)

        def moment(n):
            total = energy(u2, sh) if n == 5 else None
            a, b = fields[n // 2], fields[(n + 1) // 2]
            for k in range(3 if n < 5 else 0):
                for row in PAIR_ROWS:
                    term = a[k, row] * b[k, row]
                    total = term if total is None else total + term
            if split:
                total = jnp.where((y_at >= own_at) & (y_at < own_at + cols), total, 0.0)
            value = jnp.sum(jnp.sum(total, axis=0, keepdims=True), axis=1, keepdims=True)
            return jnp.where(lane == n, value, 0.0)

        def arrived(side):
            there = goes[side]
            in_wait(0) if side == 0 else (in_wait(1), in_wait(2))

            @pl.when(there)
            def _():
                sh_rows_copy(1 - side).wait_recv()
                for h in range(halves):
                    x_copy(1 - side, h).wait_recv()

        apply_operator(u0, u1, sh, (4, 5), valid_row)
        pack[...] = moment(0)
        arrived(1)
        apply_operator(u0, u1, sh, (6, 7, 8), valid_row)
        apply_operator(u1, u2, sh, (6, 7), valid_row)
        arrived(0)
        in_start(3)
        apply_operator(u0, u1, sh, (2, 3), valid_row)
        apply_operator(u1, u2, sh, (3, 4, 5), valid_row)

        pack[...] += moment(1) + moment(2) + moment(3) + moment(4) + moment(5)
        for number in range(2, len(reaches)):
            heard(number)
            hello(number + 1)
        cores = (1,) if split else (0, 1)
        for to in range(n_pair):
            for core in cores:
                if core == 0:
                    moment_copy(to, core).start()
                else:
                    @pl.when(m != to)
                    def _():
                        moment_copy(to, core).start()
        for j in range(3):
            basis_copy(j).start()
        in_wait(3)
        apply_operator(u0, u1, sh, (1,), valid_row)
        apply_operator(u1, u2, sh, (2,), valid_row)
        apply_operator(u2, u3, sh, PAIR_ROWS, valid_row)
        basis_copy(3).start()

        for j in range(4):
            basis[j] = fields[j][:, ROW_C:ROW_C + 2, own]
        total = pack[...]
        for pair in range(n_pair):
            @pl.when(m != pair)
            def _():
                moment_from(pair).wait_recv()
            total = total + jnp.where(m != pair, gath[pair], 0.0)
        if split:
            pack2[...] = total
            for d in range(n_inst):
                for core in (0, 1):
                    if d > 0 or core == 0:
                        across_copy(d, core).start()
            for d in range(1, n_inst):
                across_copy(d, 1).wait_recv()
                total = total + gath2[d]
        sums[...] = total

        for j in range(4):
            basis_copy(j).wait_send()
        for to in range(n_pair):
            for core in cores:
                if core == 0:
                    moment_copy(to, core).wait_send()
                else:
                    @pl.when(m != to)
                    def _():
                        moment_copy(to, core).wait_send()
        if split:
            for d in range(n_inst):
                for core in (0, 1):
                    if d > 0 or core == 0:
                        across_copy(d, core).wait_send()
        for number in range(4):
            @pl.when(inner_moves[number][3])
            def _():
                in_copy(number).wait_send()
        for h in range(halves):
            for side in range(2):
                @pl.when(goes[side])
                def _():
                    x_copy(side, h).wait_send()

            @pl.when(has_next)
            def _():
                halo_copy(0, h).wait_send()
        for piece in range(2 + 2 * halves):
            for d in range(1, n_inst):
                y_copy(piece, d).wait_send()
        for dj in offsets:
            if dj != 0:
                @pl.when(reads_me(dj))
                def _():
                    sh_copy(dj, 2, 0).wait_send()
        for side in range(2):
            @pl.when(goes[side])
            def _():
                sh_rows_copy(side).wait_send()


def combine(basis, sums, x_out, r_out, x, r, sem):
    lane = lax.broadcasted_iota(jnp.int32, sums.shape, 1)
    mu = [
        jnp.sum(jnp.where(lane == m, sums[...], 0.0), axis=1, keepdims=True) for m in range(6)
    ]
    at_x, at_r = coefficients(mu)
    moves = []
    for k in range(3):
        b = [basis[j, k] for j in range(4)]
        x[k] = at_x[0] * b[0] + at_x[1] * b[1] + at_x[2] * b[2]
        r[k] = at_r[0] * b[0] + at_r[1] * b[1] + at_r[2] * b[2] + at_r[3] * b[3]
        for q, (src, dst) in enumerate(((x, x_out), (r, r_out))):
            moves.append(pltpu.make_async_copy(src.at[k], dst.at[k], sem.at[q, k]))
            moves[-1].start()
    for move in moves:
        move.wait()


def local(n_inst, n_cell, adjoint, flux_jac, shift):
    rows, cols, nz = shift.shape
    n_i, n_v, _, ny, _ = adjoint.shape
    window = min(3, n_inst)
    wy = window * cols
    n_pair = n_cell // 2
    field = pltpu.VMEM((3, 2 * rows + 2 * HALO, wy, nz), F32)
    dma = pltpu.SemaphoreType.DMA
    out = jax.ShapeDtypeStruct((3, rows, cols, nz), F32)
    peers = max(n_inst - 1, 1)
    answers = pl.pallas_call(
        functools.partial(kernel, n_inst, n_cell, cols, window),
        out_shape=(
            jax.ShapeDtypeStruct((4, 3, rows, cols, nz), F32),
            jax.ShapeDtypeStruct((1, 128), F32),
        ),
        in_specs=[pl.BlockSpec(memory_space=pltpu.HBM)] * 3,
        out_specs=(pl.BlockSpec(memory_space=pltpu.VMEM),) * 2,
        scratch_shapes=[
            pltpu.VMEM((n_i, n_v, 2 * rows + 2, ny, nz), adjoint.dtype),
            pltpu.VMEM((n_i, n_v, 3, 2 * rows, ny, nz), flux_jac.dtype),
            pltpu.VMEM((3, 2 * rows, ny, nz), F32),
            pltpu.VMEM((peers, 3, 2 * rows, wy, nz), F32),
            field, field, field, field,
            pltpu.VMEM((2 * rows + 4, wy, nz), F32),
            pltpu.VMEM((1, 128), F32),
            pltpu.VMEM((n_pair, 1, 128), F32),
            pltpu.VMEM((1, 128), F32),
            pltpu.VMEM((n_inst, 1, 128), F32),
            dma((3,)),
            dma((3,)), dma((3,)),
            dma((2,)), dma((2, 2)),
            dma((2 * window - 1,)), dma((window, 3)),
            dma((peers, 6)), dma((peers, 6)),
            dma((4,)), dma((4,)),
            dma((2, 2)), dma((2, 2)),
            dma((4,)), dma((4,)),
            dma((n_pair, 2)), dma((n_pair,)),
            dma((n_inst, 2)), dma((n_inst,)),
            pltpu.SemaphoreType.REGULAR((7,)),
            dma((2,)), dma((2,)),
        ],
        compiler_params=pltpu.CompilerParams(
            collective_id=0, has_side_effects=True, vmem_limit_bytes=VMEM_GRANT
        ),
    )(*[pltpu.with_memory_space_constraint(a, pltpu.HBM) for a in (adjoint, flux_jac, shift)])
    return pl.pallas_call(
        combine,
        out_shape=(out, out),
        in_specs=[pl.BlockSpec(memory_space=pltpu.VMEM)] * 2,
        out_specs=(pl.BlockSpec(memory_space=pltpu.HBM),) * 2,
        scratch_shapes=[
            pltpu.VMEM((3, rows, cols, nz), F32), pltpu.VMEM((3, rows, cols, nz), F32), dma((2, 3)),
        ],
        compiler_params=pltpu.CompilerParams(vmem_limit_bytes=2 << 20),
    )(*answers)


def solution(mesh):
    placed = (
        P("inst", None, "cell", None, None),
        P("inst", None, None, "cell", None, None),
        P("cell", "inst", None),
    )
    return jax.shard_map(
        functools.partial(local, mesh.shape["inst"], mesh.shape["cell"]),
        mesh=mesh,
        in_specs=placed,
        out_specs=(P(None, "cell", "inst", None), P(None, "cell", "inst", None)),
        check_vma=False,
    )
```

```python
import functools

import jax
import jax.numpy as jnp
from jax import lax
from jax.experimental import pallas as pl
from jax.experimental.pallas import tpu as pltpu
from jax.sharding import PartitionSpec as P

ITERS = 3
LAME = 1.5
CENTER = 10.0
SPREAD = 8.0
HALO = 3
VMEM_GRANT = 40 << 20
MESH = pl.DeviceIdType.MESH
F32 = jnp.float32

ROW_A, ROW_B, ROW_C, ROW_D = 3, 4, 5, 6
PAIR_ROWS = (ROW_A, ROW_B, ROW_C, ROW_D)


def remote(src, dst, send_sem, recv_sem, device):
    return pltpu.make_async_remote_copy(
        src_ref=src,
        dst_ref=dst,
        send_sem=send_sem,
        recv_sem=recv_sem,
        device_id=device,
        device_id_type=MESH,
    )


def beside_of(v, axis, step, unit):
    n = v.shape[axis]
    if n % unit:
        unit = n
    at = lax.broadcasted_iota(jnp.int32, v.shape[:axis] + (unit,) + v.shape[axis + 1:], axis)
    seam = at == (unit - 1 if step == 1 else 0)
    tiles = [lax.slice_in_dim(v, p, p + unit, axis=axis) for p in range(0, n, unit)]
    turned = [pltpu.roll(t, unit - 1 if step == 1 else 1, axis) for t in tiles]
    outs = []
    for p in range(len(tiles)):
        beyond = p + step
        inside = 0 <= beyond < len(tiles)
        outs.append(jnp.where(seam, turned[beyond] if inside else 0.0, turned[p]))
    return jnp.concatenate(outs, axis=axis)


def apply_operator(src, dst, sh, rows, valid_row):
    up_y = functools.partial(beside_of, axis=0, step=1, unit=8)
    down_y = functools.partial(beside_of, axis=0, step=-1, unit=8)
    up_z = functools.partial(beside_of, axis=1, step=1, unit=128)
    down_z = functools.partial(beside_of, axis=1, step=-1, unit=128)

    def divergence(row):
        fields = [src[k, row] for k in range(3)]
        uy, uz = up_y(fields[1]), up_z(fields[2])
        dv = (src[0, row + 1] - fields[0]) + (uy - fields[1]) + (uz - fields[2])
        return fields, uy, uz, jnp.where(valid_row(row), dv, 0.0)

    before = {}
    for row in rows:
        if row - 1 not in before:
            before[row - 1] = divergence(row - 1)[3]
        fields, uy, uz, dv = divergence(row)
        before[row] = dv
        diag = sh[row - 1] + (6.0 - CENTER)
        shifted = [before[row - 1], down_y(dv), down_z(dv)]
        for k in range(3):
            u = fields[k]
            beside = src[k, row - 1] + src[k, row + 1]
            beside = beside + (uy if k == 1 else up_y(u)) + down_y(u)
            beside = beside + (uz if k == 2 else up_z(u)) + down_z(u)
            out = (diag * u - beside + LAME * (shifted[k] - dv)) * (1.0 / SPREAD)
            dst[k, row] = jnp.where(valid_row(row), out, 0.0)


def energy(src, sh):
    total = None
    for row in PAIR_ROWS:
        dv = None
        for k in range(3):
            v = src[k, row]
            above = (
                src[k, row + 1],
                beside_of(v, 0, 1, 8),
                beside_of(v, 1, 1, 128),
            )
            step = above[k] - v
            dv = step if dv is None else dv + step
            diag = sh[row - 1] + (6.0 - CENTER)
            term = v * (diag * v - 2.0 * (above[0] + above[1] + above[2]))
            total = term if total is None else total + term
        total = total + LAME * (dv * dv)
    return total * (1.0 / SPREAD)


def coefficients(mu):
    def inner(a, b, skip=0):
        total = None
        for p, x in enumerate(a):
            for q, y in enumerate(b):
                if x is None or y is None:
                    continue
                term = x * y * mu[p + q]
                total = term if total is None else total + term
        return total

    def times(a):
        return [
            (CENTER * a[j] if j < len(a) else 0.0) + (SPREAD * a[j - 1] if j > 0 else 0.0)
            for j in range(len(a) + 1)
        ]

    one = jnp.ones_like(mu[0])
    solution_at, residual, direction = [], [one], [one]
    norm_now = mu[0]
    for sweep in range(ITERS):
        image = times(direction)
        alpha = norm_now / inner(direction, image)
        solution_at = [
            (solution_at[j] if j < len(solution_at) else 0.0) + alpha * direction[j]
            for j in range(len(direction))
        ]
        residual = [
            (residual[j] if j < len(residual) else 0.0) - alpha * image[j]
            for j in range(len(image))
        ]
        if sweep + 1 < ITERS:
            norm_next = inner(residual, residual)
            ratio = norm_next / norm_now
            direction = [
                residual[j] + (ratio * direction[j] if j < len(direction) else 0.0)
                for j in range(len(residual))
            ]
            norm_now = norm_next
    return solution_at, residual


def kernel(
    n_inst, n_cell, cols, window,
    adj_hbm, flux_hbm, shift_hbm, basis, sums,
    adj, flux, part, got, u0, u1, u2, u3, sh, pack, gath, pack2, gath2,
    load_sem, give_send, give_recv, halo_send, halo_recv, sh_send, sh_recv,
    y_send, y_recv, in_send, in_recv, x_send, x_recv, b_send, b_recv,
    g_send, g_recv, h_send, h_recv, near, shx_send, shx_recv,
):
    i, c = lax.axis_index("inst"), lax.axis_index("cell")
    n_pair = n_cell // 2
    m = c // 2
    wy = window * cols
    n_v = adj.shape[1]
    nv = adj.shape[0] * n_v
    ny, nz = adj.shape[3], adj.shape[4]
    halves = 2 if nz % 256 == 0 else 1
    split = window < n_inst
    has_prev, has_next = m > 0, m < n_pair - 1
    barrier = pltpu.get_barrier_semaphore()

    def lanes(h):
        return slice(h * (nz // halves), (h + 1) * (nz // halves))

    def start_of(j):
        return jnp.clip(j - 1, 0, n_inst - window)

    def slot_at(j, who):
        return jnp.clip(who - start_of(j), 0, window - 1)

    own_at = pl.multiple_of((i - start_of(i)) * cols, cols)
    own = pl.ds(own_at, cols)
    offsets = range(-(window - 1), window)

    def reads_me(dj):
        j = i + dj
        first = start_of(j)
        return (j >= 0) & (j < n_inst) & (i >= first) & (i < first + window)

    def read_by_me(dj):
        first = start_of(i)
        return (i + dj >= first) & (i + dj < first + window)

    def tell(condition, device):
        if condition is True:
            pl.semaphore_signal(barrier, inc=1, device_id=device, device_id_type=MESH)
        else:
            @pl.when(condition)
            def _():
                pl.semaphore_signal(barrier, inc=1, device_id=device, device_id_type=MESH)

    def one_if(condition):
        return jnp.where(condition, 1, 0)

    def sh_copy(dj, block, dc):
        j = i + dj
        slot = slot_at(j, i)
        at = pl.multiple_of(slot * cols, cols)
        return remote(
            shift_hbm, sh.at[2 * block:2 * block + 2, pl.ds(at, cols)],
            sh_send.at[dj + window - 1], sh_recv.at[slot, block], (j, c + dc),
        )

    def moment_copy(to, core):
        return remote(
            pack, gath.at[m], g_send.at[to, core], g_recv.at[m], (i, 2 * to + core)
        )

    def moment_from(pair):
        return remote(pack, gath.at[pair], g_send.at[0, 0], g_recv.at[pair], (i, c))

    def across_copy(d, core):
        to = lax.rem(i + d, n_inst)
        return remote(
            pack2, gath2.at[d], h_send.at[d, core], h_recv.at[d], (to, 2 * m + core)
        )

    def basis_copy(j):
        source = (u0, u1, u2, u3)[j]
        return remote(
            source.at[:, ROW_A:ROW_C, own], basis.at[j], b_send.at[j], b_recv.at[j], (i, c - 1)
        )

    def halo_copy(side, h):
        if side == 0:
            return remote(
                adj.at[:, :, 4, :, lanes(h)], adj.at[:, :, 0, :, lanes(h)],
                halo_send.at[h], halo_recv.at[0, h], (i, c + 2),
            )
        return remote(
            adj_hbm.at[:, :, 0, :, lanes(h)], adj.at[:, :, 5, :, lanes(h)],
            halo_send.at[h], halo_recv.at[1, h], (i, c - 1),
        )

    def give_copy(number):
        src, dst = (
            (adj_hbm, adj.at[:, :, 1:3]),
            (flux_hbm.at[:, :, :, 1], flux.at[:, :, :, 1]),
            (flux_hbm.at[:, :, :, 0], flux.at[:, :, :, 0]),
        )[number]
        return remote(src, dst, give_send.at[number], give_recv.at[number], (i, c + 1))

    @pl.when(c % 2 == 0)
    def even():
        if split:
            for d in range(n_inst):
                tell(True, (lax.rem(i + d, n_inst), c + 1))
        else:
            tell(True, (i, c + 1))
        expected = one_if(has_prev)
        for dj in offsets:
            expected = expected + one_if(reads_me(dj))
        pl.semaphore_wait(barrier, expected)

        for h in range(halves):
            @pl.when(has_prev)
            def _():
                halo_copy(1, h).start()
        for number in range(3):
            give_copy(number).start()
        for dj in offsets:
            @pl.when(reads_me(dj))
            def _():
                sh_copy(dj, 1, 1).start()

        for number in range(3):
            give_copy(number).wait_send()
        for h in range(halves):
            @pl.when(has_prev)
            def _():
                halo_copy(1, h).wait_send()
        for dj in offsets:
            @pl.when(reads_me(dj))
            def _():
                sh_copy(dj, 1, 1).wait_send()

        for j in range(4):
            remote(basis.at[j], basis.at[j], b_send.at[j], b_recv.at[j], (i, c)).wait_recv()
        total = None
        if split:
            for d in range(n_inst):
                across_copy(d, 0).wait_recv()
                total = gath2[d] if total is None else total + gath2[d]
        else:
            for d in range(n_pair):
                moment_from(d).wait_recv()
                total = gath[d] if total is None else total + gath[d]
        sums[...] = total

    @pl.when(c % 2 == 1)
    def odd():
        tell(has_prev, (i, c - 2))
        tell(has_next, (i, c + 1))
        tell(has_next, (i, c + 2))
        for dj in offsets:
            tell(read_by_me(dj), (i + dj, c - 1))
        for d in range(1, n_inst):
            tell(True, (lax.rem(i + d, n_inst), c))
        loads = [
            pltpu.make_async_copy(adj_hbm, adj.at[:, :, 3:5], load_sem.at[0]),
            pltpu.make_async_copy(flux_hbm, flux.at[:, :, :, 2:4], load_sem.at[1]),
            pltpu.make_async_copy(shift_hbm, sh.at[4:6, own], load_sem.at[2]),
        ]
        for load in loads:
            load.start()
        expected = (n_inst - 1) + one_if(has_prev) + one_if(has_next) + (n_inst if split else 1)
        pl.semaphore_wait(barrier, expected)

        reaches = [r for r in (1, 2, 4, 8, 16, 32, 64) if r < n_pair]

        def inside(dm):
            return (m + dm >= 0) & (m + dm < n_pair)

        def hello(number):
            if number < len(reaches):
                for dm in (-reaches[number], reaches[number]):
                    @pl.when(inside(dm))
                    def _():
                        pl.semaphore_signal(
                            near.at[number], inc=1, device_id=(i, c + 2 * dm), device_id_type=MESH
                        )

        def heard(number):
            if number < len(reaches):
                count = 0
                for dm in (-reaches[number], reaches[number]):
                    count = count + one_if(inside(dm))
                pl.semaphore_wait(near.at[number], count)

        loads[0].wait()
        for h in range(halves):
            @pl.when(has_next)
            def _():
                halo_copy(0, h).start()
        hello(0)
        for dj in offsets:
            if dj != 0:
                @pl.when(reads_me(dj))
                def _():
                    sh_copy(dj, 2, 0).start()

        @pl.when(jnp.logical_not(has_prev))
        def _():
            adj[:, :, 0] = jnp.zeros_like(adj[:, :, 0])
            sh[0:2] = jnp.zeros_like(sh[0:2])
            u0[:, 0:3] = jnp.zeros_like(u0[:, 0:3])

        @pl.when(jnp.logical_not(has_next))
        def _():
            adj[:, :, 5] = jnp.zeros_like(adj[:, :, 5])
            sh[6:8] = jnp.zeros_like(sh[6:8])
            u0[:, 7:10] = jnp.zeros_like(u0[:, 7:10])

        def y_copy(piece, d):
            j = lax.rem(i + d, n_inst)
            at = pl.multiple_of(start_of(j) * cols, cols)
            if piece < 2:
                row, ls = 2 - piece, slice(None)
            else:
                row, ls = (0, 3)[piece % 2], lanes(piece // 2 - 1)
            return remote(
                part.at[:, row, pl.ds(at, wy), ls], got.at[d - 1, :, row, :, ls],
                y_send.at[d - 1, piece], y_recv.at[d - 1, piece], (j, c),
            )

        chunks = [slice(y0, y0 + 16) for y0 in range(0, ny, 16)]

        def whole_terms(row):
            for ys in chunks:
                total = [None] * 3
                for v in range(nv):
                    a, b = v // n_v, v % n_v
                    step = adj[a, b, row + 2, ys].astype(F32) - adj[a, b, row, ys].astype(F32)
                    for k in range(3):
                        t = flux[a, b, k, row, ys].astype(F32) * step
                        total[k] = t if total[k] is None else total[k] + t
                for k in range(3):
                    part[k, row, ys] = total[k]

        def own_terms(row, beside, sign):
            for ys in chunks:
                total = [None] * 3
                for v in range(nv):
                    a, b = v // n_v, v % n_v
                    other = adj[a, b, beside, ys].astype(F32)
                    for k in range(3):
                        t = flux[a, b, k, row, ys].astype(F32) * other
                        total[k] = t if total[k] is None else total[k] + t
                for k in range(3):
                    part[k, row, ys] = total[k] if sign > 0 else -total[k]

        def halo_terms(row, beside, sign, h):
            ls = lanes(h)
            for ys in chunks:
                total = [part[k, row, ys, ls] for k in range(3)]
                for v in range(nv):
                    a, b = v // n_v, v % n_v
                    other = adj[a, b, beside, ys, ls].astype(F32)
                    for k in range(3):
                        t = flux[a, b, k, row, ys, ls].astype(F32) * other
                        total[k] = total[k] + t if sign > 0 else total[k] - t
                for k in range(3):
                    part[k, row, ys, ls] = total[k]

        goes = (has_prev, has_next)

        def sh_rows_copy(side):
            src, dst = ((2, 6), (4, 0))[side]
            return remote(
                sh.at[src:src + 2], sh.at[dst:dst + 2],
                shx_send.at[side], shx_recv.at[side], (i, c + 2 * (2 * side - 1)),
            )

        def sh_landed(slot, block):
            at = sh.at[2 * block:2 * block + 2, pl.ds(slot * cols, cols)]
            remote(at, at, sh_send.at[0], sh_recv.at[slot, block], (i, c)).wait_recv()

        def shift_rows():
            loads[2].wait()
            for slot in range(window):
                sh_landed(slot, 1)

                @pl.when(start_of(i) + slot != i)
                def _():
                    sh_landed(slot, 2)
            for side in range(2):
                @pl.when(goes[side])
                def _():
                    sh_rows_copy(side).start()

        loads[1].wait()
        own_terms(3, 3, -1)
        give_copy(0).wait_recv()
        whole_terms(2)
        for d in range(1, n_inst):
            y_copy(0, d).start()
        give_copy(1).wait_recv()
        whole_terms(1)
        for d in range(1, n_inst):
            y_copy(1, d).start()
        give_copy(2).wait_recv()
        own_terms(0, 2, 1)

        for h in range(halves):
            @pl.when(has_prev)
            def _():
                halo_copy(0, h).wait_recv()
            halo_terms(0, 0, -1, h)
            for d in range(1, n_inst):
                y_copy(2 + 2 * h, d).start()

            @pl.when(has_next)
            def _():
                halo_copy(1, h).wait_recv()
            halo_terms(3, 5, 1, h)
            for d in range(1, n_inst):
                y_copy(3 + 2 * h, d).start()
            if h == 0:
                shift_rows()

        my_at = pl.multiple_of(start_of(i) * cols, cols)

        def add_up(piece):
            for d in range(1, n_inst):
                y_copy(piece, d).wait_recv()
            if piece < 2:
                row, ls = 2 - piece, slice(None)
            else:
                row, ls = (0, 3)[piece % 2], lanes(piece // 2 - 1)
            for k in range(3):
                total = part[k, row, pl.ds(my_at, wy), ls]
                for d in range(1, n_inst):
                    total = total + got[d - 1, k, row, :, ls]
                u0[k, ROW_A + row, :, ls] = total

        inner_moves = (
            (5, 1, 1, has_next),
            (5, 9, -1, has_prev),
            (4, 8, -1, has_prev),
            (4, 0, 1, has_next),
        )

        def in_copy(number):
            src, dst, dm, _ = inner_moves[number]
            return remote(
                u0.at[:, src], u0.at[:, dst], in_send.at[number], in_recv.at[number], (i, c + 2 * dm)
            )

        def in_start(number):
            @pl.when(inner_moves[number][3])
            def _():
                in_copy(number).start()

        def in_wait(number):
            arrives = has_prev if inner_moves[number][2] == 1 else has_next

            @pl.when(arrives)
            def _():
                in_copy(number).wait_recv()

        def x_copy(side, h):
            src, dst, dm = ((ROW_A, 7, -1), (ROW_D, 2, 1))[side]
            return remote(
                u0.at[:, src, :, lanes(h)], u0.at[:, dst, :, lanes(h)],
                x_send.at[side, h], x_recv.at[side, h], (i, c + 2 * dm),
            )

        add_up(0)
        in_start(1)
        in_start(0)
        heard(0)
        hello(1)
        add_up(1)
        in_start(2)
        for h in range(halves):
            for side in range(2):
                add_up(2 + 2 * h + side)

                @pl.when(goes[side])
                def _():
                    x_copy(side, h).start()

        heard(1)
        hello(2)

        shape = (wy, nz)
        y_at = lax.broadcasted_iota(jnp.int32, shape, 0)

        def valid_row(row):
            if row in PAIR_ROWS:
                return True
            return has_prev if row < ROW_A else has_next

        fields = (u0, u1, u2, u3)
        lane = lax.broadcasted_iota(jnp.int32, (1, 128), 1)

        def moment(n):
            total = energy(u2, sh) if n == 5 else None
            a, b = fields[n // 2], fields[(n + 1) // 2]
            for k in range(3 if n < 5 else 0):
                for row in PAIR_ROWS:
                    term = a[k, row] * b[k, row]
                    total = term if total is None else total + term
            if split:
                total = jnp.where((y_at >= own_at) & (y_at < own_at + cols), total, 0.0)
            value = jnp.sum(jnp.sum(total, axis=0, keepdims=True), axis=1, keepdims=True)
            return jnp.where(lane == n, value, 0.0)

        def arrived(side):
            there = goes[side]
            in_wait(0) if side == 0 else (in_wait(1), in_wait(2))

            @pl.when(there)
            def _():
                sh_rows_copy(1 - side).wait_recv()
                for h in range(halves):
                    x_copy(1 - side, h).wait_recv()

        apply_operator(u0, u1, sh, (4, 5), valid_row)
        pack[...] = moment(0)
        arrived(1)
        apply_operator(u0, u1, sh, (6, 7, 8), valid_row)
        apply_operator(u1, u2, sh, (6, 7), valid_row)
        arrived(0)
        in_start(3)
        apply_operator(u0, u1, sh, (2, 3), valid_row)
        apply_operator(u1, u2, sh, (3, 4, 5), valid_row)

        pack[...] += moment(1) + moment(2) + moment(3) + moment(4) + moment(5)
        for number in range(2, len(reaches)):
            heard(number)
            hello(number + 1)
        cores = (1,) if split else (0, 1)
        for to in range(n_pair):
            for core in cores:
                if core == 0:
                    moment_copy(to, core).start()
                else:
                    @pl.when(m != to)
                    def _():
                        moment_copy(to, core).start()
        for j in range(3):
            basis_copy(j).start()
        in_wait(3)
        apply_operator(u0, u1, sh, (1,), valid_row)
        apply_operator(u1, u2, sh, (2,), valid_row)
        apply_operator(u2, u3, sh, PAIR_ROWS, valid_row)
        basis_copy(3).start()

        for j in range(4):
            basis[j] = fields[j][:, ROW_C:ROW_C + 2, own]
        total = pack[...]
        for pair in range(n_pair):
            @pl.when(m != pair)
            def _():
                moment_from(pair).wait_recv()
            total = total + jnp.where(m != pair, gath[pair], 0.0)
        if split:
            pack2[...] = total
            for d in range(n_inst):
                for core in (0, 1):
                    if d > 0 or core == 0:
                        across_copy(d, core).start()
            for d in range(1, n_inst):
                across_copy(d, 1).wait_recv()
                total = total + gath2[d]
        sums[...] = total

        for j in range(4):
            basis_copy(j).wait_send()
        for to in range(n_pair):
            for core in cores:
                if core == 0:
                    moment_copy(to, core).wait_send()
                else:
                    @pl.when(m != to)
                    def _():
                        moment_copy(to, core).wait_send()
        if split:
            for d in range(n_inst):
                for core in (0, 1):
                    if d > 0 or core == 0:
                        across_copy(d, core).wait_send()
        for number in range(4):
            @pl.when(inner_moves[number][3])
            def _():
                in_copy(number).wait_send()
        for h in range(halves):
            for side in range(2):
                @pl.when(goes[side])
                def _():
                    x_copy(side, h).wait_send()

            @pl.when(has_next)
            def _():
                halo_copy(0, h).wait_send()
        for piece in range(2 + 2 * halves):
            for d in range(1, n_inst):
                y_copy(piece, d).wait_send()
        for dj in offsets:
            if dj != 0:
                @pl.when(reads_me(dj))
                def _():
                    sh_copy(dj, 2, 0).wait_send()
        for side in range(2):
            @pl.when(goes[side])
            def _():
                sh_rows_copy(side).wait_send()


def combine(basis, sums, x_out, r_out, x, r, sem):
    lane = lax.broadcasted_iota(jnp.int32, sums.shape, 1)
    mu = [
        jnp.sum(jnp.where(lane == m, sums[...], 0.0), axis=1, keepdims=True) for m in range(6)
    ]
    at_x, at_r = coefficients(mu)
    moves = []
    for k in range(3):
        b = [basis[j, k] for j in range(4)]
        x[k] = at_x[0] * b[0] + at_x[1] * b[1] + at_x[2] * b[2]
        r[k] = at_r[0] * b[0] + at_r[1] * b[1] + at_r[2] * b[2] + at_r[3] * b[3]
        for q, (src, dst) in enumerate(((x, x_out), (r, r_out))):
            moves.append(pltpu.make_async_copy(src.at[k], dst.at[k], sem.at[q, k]))
            moves[-1].start()
    for move in moves:
        move.wait()


def local(n_inst, n_cell, adjoint, flux_jac, shift):
    rows, cols, nz = shift.shape
    n_i, n_v, _, ny, _ = adjoint.shape
    window = min(3, n_inst)
    wy = window * cols
    n_pair = n_cell // 2
    field = pltpu.VMEM((3, 2 * rows + 2 * HALO, wy, nz), F32)
    dma = pltpu.SemaphoreType.DMA
    out = jax.ShapeDtypeStruct((3, rows, cols, nz), F32)
    peers = max(n_inst - 1, 1)
    answers = pl.pallas_call(
        functools.partial(kernel, n_inst, n_cell, cols, window),
        out_shape=(
            jax.ShapeDtypeStruct((4, 3, rows, cols, nz), F32),
            jax.ShapeDtypeStruct((1, 128), F32),
        ),
        in_specs=[pl.BlockSpec(memory_space=pltpu.HBM)] * 3,
        out_specs=(pl.BlockSpec(memory_space=pltpu.VMEM),) * 2,
        scratch_shapes=[
            pltpu.VMEM((n_i, n_v, 2 * rows + 2, ny, nz), adjoint.dtype),
            pltpu.VMEM((n_i, n_v, 3, 2 * rows, ny, nz), flux_jac.dtype),
            pltpu.VMEM((3, 2 * rows, ny, nz), F32),
            pltpu.VMEM((peers, 3, 2 * rows, wy, nz), F32),
            field, field, field, field,
            pltpu.VMEM((2 * rows + 4, wy, nz), F32),
            pltpu.VMEM((1, 128), F32),
            pltpu.VMEM((n_pair, 1, 128), F32),
            pltpu.VMEM((1, 128), F32),
            pltpu.VMEM((n_inst, 1, 128), F32),
            dma((3,)),
            dma((3,)), dma((3,)),
            dma((2,)), dma((2, 2)),
            dma((2 * window - 1,)), dma((window, 3)),
            dma((peers, 6)), dma((peers, 6)),
            dma((4,)), dma((4,)),
            dma((2, 2)), dma((2, 2)),
            dma((4,)), dma((4,)),
            dma((n_pair, 2)), dma((n_pair,)),
            dma((n_inst, 2)), dma((n_inst,)),
            pltpu.SemaphoreType.REGULAR((7,)),
            dma((2,)), dma((2,)),
        ],
        compiler_params=pltpu.CompilerParams(
            collective_id=0, has_side_effects=True, vmem_limit_bytes=VMEM_GRANT
        ),
    )(*[pltpu.with_memory_space_constraint(a, pltpu.HBM) for a in (adjoint, flux_jac, shift)])
    return pl.pallas_call(
        combine,
        out_shape=(out, out),
        in_specs=[pl.BlockSpec(memory_space=pltpu.VMEM)] * 2,
        out_specs=(pl.BlockSpec(memory_space=pltpu.HBM),) * 2,
        scratch_shapes=[
            pltpu.VMEM((3, rows, cols, nz), F32), pltpu.VMEM((3, rows, cols, nz), F32), dma((2, 3)),
        ],
        compiler_params=pltpu.CompilerParams(vmem_limit_bytes=2 << 20),
    )(*answers)


def solution(mesh):
    placed = (
        P("inst", None, "cell", None, None),
        P("inst", None, None, "cell", None, None),
        P("cell", "inst", None),
    )
    return jax.shard_map(
        functools.partial(local, mesh.shape["inst"], mesh.shape["cell"]),
        mesh=mesh,
        in_specs=placed,
        out_specs=(P(None, "cell", "inst", None), P(None, "cell", "inst", None)),
        check_vma=False,
    )
```

```python
import functools

import jax
import jax.numpy as jnp
from jax import lax
from jax.experimental import pallas as pl
from jax.experimental.pallas import tpu as pltpu
from jax.sharding import PartitionSpec as P

ITERS = 3
LAME = 1.5
CENTER = 10.0
SPREAD = 8.0
HALO = 3
VMEM_GRANT = 40 << 20
MESH = pl.DeviceIdType.MESH
F32 = jnp.float32

ROW_A, ROW_B, ROW_C, ROW_D = 3, 4, 5, 6
PAIR_ROWS = (ROW_A, ROW_B, ROW_C, ROW_D)


def remote(src, dst, send_sem, recv_sem, device):
    return pltpu.make_async_remote_copy(
        src_ref=src,
        dst_ref=dst,
        send_sem=send_sem,
        recv_sem=recv_sem,
        device_id=device,
        device_id_type=MESH,
    )


def beside_of(v, axis, step, unit):
    n = v.shape[axis]
    if n % unit:
        unit = n
    at = lax.broadcasted_iota(jnp.int32, v.shape[:axis] + (unit,) + v.shape[axis + 1:], axis)
    seam = at == (unit - 1 if step == 1 else 0)
    tiles = [lax.slice_in_dim(v, p, p + unit, axis=axis) for p in range(0, n, unit)]
    turned = [pltpu.roll(t, unit - 1 if step == 1 else 1, axis) for t in tiles]
    outs = []
    for p in range(len(tiles)):
        beyond = p + step
        inside = 0 <= beyond < len(tiles)
        outs.append(jnp.where(seam, turned[beyond] if inside else 0.0, turned[p]))
    return jnp.concatenate(outs, axis=axis)


def apply_operator(src, dst, sh, rows, valid_row):
    up_y = functools.partial(beside_of, axis=0, step=1, unit=8)
    down_y = functools.partial(beside_of, axis=0, step=-1, unit=8)
    up_z = functools.partial(beside_of, axis=1, step=1, unit=128)
    down_z = functools.partial(beside_of, axis=1, step=-1, unit=128)

    def divergence(row):
        fields = [src[k, row] for k in range(3)]
        uy, uz = up_y(fields[1]), up_z(fields[2])
        dv = (src[0, row + 1] - fields[0]) + (uy - fields[1]) + (uz - fields[2])
        dv = dv * (LAME / SPREAD)
        return fields, uy, uz, dv if valid_row(row) is True else jnp.where(valid_row(row), dv, 0.0)

    before = {}
    for row in rows:
        if row - 1 not in before:
            before[row - 1] = divergence(row - 1)[3]
        fields, uy, uz, dv = divergence(row)
        before[row] = dv
        diag = (sh[row - 1] + (6.0 - CENTER)) * (1.0 / SPREAD)
        shifted = [before[row - 1], down_y(dv), down_z(dv)]
        for k in range(3):
            u = fields[k]
            beside = src[k, row - 1] + src[k, row + 1]
            beside = beside + (uy if k == 1 else up_y(u)) + down_y(u)
            beside = beside + (uz if k == 2 else up_z(u)) + down_z(u)
            out = diag * u - beside * (1.0 / SPREAD) + (shifted[k] - dv)
            dst[k, row] = out if valid_row(row) is True else jnp.where(valid_row(row), out, 0.0)


def energy(src, sh):
    total = None
    for row in PAIR_ROWS:
        dv = None
        for k in range(3):
            v = src[k, row]
            above = (
                src[k, row + 1],
                beside_of(v, 0, 1, 8),
                beside_of(v, 1, 1, 128),
            )
            step = above[k] - v
            dv = step if dv is None else dv + step
            diag = sh[row - 1] + (6.0 - CENTER)
            term = v * (diag * v - 2.0 * (above[0] + above[1] + above[2]))
            total = term if total is None else total + term
        total = total + LAME * (dv * dv)
    return total * (1.0 / SPREAD)


def coefficients(mu):
    def inner(a, b, skip=0):
        total = None
        for p, x in enumerate(a):
            for q, y in enumerate(b):
                if x is None or y is None:
                    continue
                term = x * y * mu[p + q]
                total = term if total is None else total + term
        return total

    def times(a):
        return [
            (CENTER * a[j] if j < len(a) else 0.0) + (SPREAD * a[j - 1] if j > 0 else 0.0)
            for j in range(len(a) + 1)
        ]

    one = jnp.ones_like(mu[0])
    solution_at, residual, direction = [], [one], [one]
    norm_now = mu[0]
    for sweep in range(ITERS):
        image = times(direction)
        alpha = norm_now / inner(direction, image)
        solution_at = [
            (solution_at[j] if j < len(solution_at) else 0.0) + alpha * direction[j]
            for j in range(len(direction))
        ]
        residual = [
            (residual[j] if j < len(residual) else 0.0) - alpha * image[j]
            for j in range(len(image))
        ]
        if sweep + 1 < ITERS:
            norm_next = inner(residual, residual)
            ratio = norm_next / norm_now
            direction = [
                residual[j] + (ratio * direction[j] if j < len(direction) else 0.0)
                for j in range(len(residual))
            ]
            norm_now = norm_next
    return solution_at, residual


def kernel(
    n_inst, n_cell, cols, window,
    adj_hbm, flux_hbm, shift_hbm, basis, sums,
    adj, flux, part, got, u0, u1, u2, u3, sh, pack, gath, pack2, gath2,
    load_sem, give_send, give_recv, halo_send, halo_recv, sh_send, sh_recv,
    y_send, y_recv, in_send, in_recv, x_send, x_recv, b_send, b_recv,
    g_send, g_recv, h_send, h_recv, near, shx_send, shx_recv,
):
    i, c = lax.axis_index("inst"), lax.axis_index("cell")
    n_pair = n_cell // 2
    m = c // 2
    wy = window * cols
    n_v = adj.shape[1]
    nv = adj.shape[0] * n_v
    ny, nz = adj.shape[3], adj.shape[4]
    halves = 2 if nz % 256 == 0 else 1
    split = window < n_inst
    has_prev, has_next = m > 0, m < n_pair - 1
    barrier = pltpu.get_barrier_semaphore()

    def lanes(h):
        return slice(h * (nz // halves), (h + 1) * (nz // halves))

    def start_of(j):
        return jnp.clip(j - 1, 0, n_inst - window)

    def slot_at(j, who):
        return jnp.clip(who - start_of(j), 0, window - 1)

    own_at = pl.multiple_of((i - start_of(i)) * cols, cols)
    own = pl.ds(own_at, cols)
    offsets = range(-(window - 1), window)

    def reads_me(dj):
        j = i + dj
        first = start_of(j)
        return (j >= 0) & (j < n_inst) & (i >= first) & (i < first + window)

    def read_by_me(dj):
        first = start_of(i)
        return (i + dj >= first) & (i + dj < first + window)

    def tell(condition, device):
        if condition is True:
            pl.semaphore_signal(barrier, inc=1, device_id=device, device_id_type=MESH)
        else:
            @pl.when(condition)
            def _():
                pl.semaphore_signal(barrier, inc=1, device_id=device, device_id_type=MESH)

    def one_if(condition):
        return jnp.where(condition, 1, 0)

    def sh_copy(dj, block, dc):
        j = i + dj
        slot = slot_at(j, i)
        at = pl.multiple_of(slot * cols, cols)
        return remote(
            shift_hbm, sh.at[2 * block:2 * block + 2, pl.ds(at, cols)],
            sh_send.at[dj + window - 1], sh_recv.at[slot, block], (j, c + dc),
        )

    def moment_copy(to, core):
        return remote(
            pack, gath.at[m], g_send.at[to, core], g_recv.at[m], (i, 2 * to + core)
        )

    def moment_from(pair):
        return remote(pack, gath.at[pair], g_send.at[0, 0], g_recv.at[pair], (i, c))

    def across_copy(d, core):
        to = lax.rem(i + d, n_inst)
        return remote(
            pack2, gath2.at[d], h_send.at[d, core], h_recv.at[d], (to, 2 * m + core)
        )

    def basis_copy(j):
        source = (u0, u1, u2, u3)[j]
        return remote(
            source.at[:, ROW_A:ROW_C, own], basis.at[j], b_send.at[j], b_recv.at[j], (i, c - 1)
        )

    def halo_copy(side, h):
        if side == 0:
            return remote(
                adj.at[:, :, 4, :, lanes(h)], adj.at[:, :, 0, :, lanes(h)],
                halo_send.at[h], halo_recv.at[0, h], (i, c + 2),
            )
        return remote(
            adj_hbm.at[:, :, 0, :, lanes(h)], adj.at[:, :, 5, :, lanes(h)],
            halo_send.at[h], halo_recv.at[1, h], (i, c - 1),
        )

    def give_copy(number):
        src, dst = (
            (adj_hbm, adj.at[:, :, 1:3]),
            (flux_hbm.at[:, :, :, 1], flux.at[:, :, :, 1]),
            (flux_hbm.at[:, :, :, 0], flux.at[:, :, :, 0]),
        )[number]
        return remote(src, dst, give_send.at[number], give_recv.at[number], (i, c + 1))

    @pl.when(c % 2 == 0)
    def even():
        if split:
            for d in range(n_inst):
                tell(True, (lax.rem(i + d, n_inst), c + 1))
        else:
            tell(True, (i, c + 1))
        expected = one_if(has_prev)
        for dj in offsets:
            expected = expected + one_if(reads_me(dj))
        pl.semaphore_wait(barrier, expected)

        for h in range(halves):
            @pl.when(has_prev)
            def _():
                halo_copy(1, h).start()
        for number in range(3):
            give_copy(number).start()
        for dj in offsets:
            @pl.when(reads_me(dj))
            def _():
                sh_copy(dj, 1, 1).start()

        for number in range(3):
            give_copy(number).wait_send()
        for h in range(halves):
            @pl.when(has_prev)
            def _():
                halo_copy(1, h).wait_send()
        for dj in offsets:
            @pl.when(reads_me(dj))
            def _():
                sh_copy(dj, 1, 1).wait_send()

        for j in range(4):
            remote(basis.at[j], basis.at[j], b_send.at[j], b_recv.at[j], (i, c)).wait_recv()
        total = None
        if split:
            for d in range(n_inst):
                across_copy(d, 0).wait_recv()
                total = gath2[d] if total is None else total + gath2[d]
        else:
            for d in range(n_pair):
                moment_from(d).wait_recv()
                total = gath[d] if total is None else total + gath[d]
        sums[...] = total

    @pl.when(c % 2 == 1)
    def odd():
        tell(has_prev, (i, c - 2))
        tell(has_next, (i, c + 1))
        tell(has_next, (i, c + 2))
        for dj in offsets:
            tell(read_by_me(dj), (i + dj, c - 1))
        for d in range(1, n_inst):
            tell(True, (lax.rem(i + d, n_inst), c))
        loads = [
            pltpu.make_async_copy(adj_hbm, adj.at[:, :, 3:5], load_sem.at[0]),
            pltpu.make_async_copy(flux_hbm, flux.at[:, :, :, 2:4], load_sem.at[1]),
            pltpu.make_async_copy(shift_hbm, sh.at[4:6, own], load_sem.at[2]),
        ]
        for load in loads:
            load.start()
        expected = (n_inst - 1) + one_if(has_prev) + one_if(has_next) + (n_inst if split else 1)
        pl.semaphore_wait(barrier, expected)

        reaches = [r for r in (1, 2, 4, 8, 16, 32, 64) if r < n_pair]

        def inside(dm):
            return (m + dm >= 0) & (m + dm < n_pair)

        def hello(number):
            if number < len(reaches):
                for dm in (-reaches[number], reaches[number]):
                    @pl.when(inside(dm))
                    def _():
                        pl.semaphore_signal(
                            near.at[number], inc=1, device_id=(i, c + 2 * dm), device_id_type=MESH
                        )

        def heard(number):
            if number < len(reaches):
                count = 0
                for dm in (-reaches[number], reaches[number]):
                    count = count + one_if(inside(dm))
                pl.semaphore_wait(near.at[number], count)

        loads[0].wait()
        for h in range(halves):
            @pl.when(has_next)
            def _():
                halo_copy(0, h).start()
        hello(0)
        for dj in offsets:
            if dj != 0:
                @pl.when(reads_me(dj))
                def _():
                    sh_copy(dj, 2, 0).start()

        @pl.when(jnp.logical_not(has_prev))
        def _():
            adj[:, :, 0] = jnp.zeros_like(adj[:, :, 0])
            sh[0:2] = jnp.zeros_like(sh[0:2])
            u0[:, 0:3] = jnp.zeros_like(u0[:, 0:3])

        @pl.when(jnp.logical_not(has_next))
        def _():
            adj[:, :, 5] = jnp.zeros_like(adj[:, :, 5])
            sh[6:8] = jnp.zeros_like(sh[6:8])
            u0[:, 7:10] = jnp.zeros_like(u0[:, 7:10])

        def y_copy(piece, d):
            j = lax.rem(i + d, n_inst)
            at = pl.multiple_of(start_of(j) * cols, cols)
            if piece < 2:
                row, ls = 2 - piece, slice(None)
            else:
                row, ls = (0, 3)[piece % 2], lanes(piece // 2 - 1)
            return remote(
                part.at[:, row, pl.ds(at, wy), ls], got.at[d - 1, :, row, :, ls],
                y_send.at[d - 1, piece], y_recv.at[d - 1, piece], (j, c),
            )

        chunks = [slice(y0, y0 + 16) for y0 in range(0, ny, 16)]

        def whole_terms(row):
            for ys in chunks:
                total = [None] * 3
                for v in range(nv):
                    a, b = v // n_v, v % n_v
                    step = adj[a, b, row + 2, ys].astype(F32) - adj[a, b, row, ys].astype(F32)
                    for k in range(3):
                        t = flux[a, b, k, row, ys].astype(F32) * step
                        total[k] = t if total[k] is None else total[k] + t
                for k in range(3):
                    part[k, row, ys] = total[k]

        def own_terms(row, beside, sign):
            for ys in chunks:
                total = [None] * 3
                for v in range(nv):
                    a, b = v // n_v, v % n_v
                    other = adj[a, b, beside, ys].astype(F32)
                    for k in range(3):
                        t = flux[a, b, k, row, ys].astype(F32) * other
                        total[k] = t if total[k] is None else total[k] + t
                for k in range(3):
                    part[k, row, ys] = total[k] if sign > 0 else -total[k]

        def halo_terms(row, beside, sign, h):
            ls = lanes(h)
            for ys in chunks:
                total = [part[k, row, ys, ls] for k in range(3)]
                for v in range(nv):
                    a, b = v // n_v, v % n_v
                    other = adj[a, b, beside, ys, ls].astype(F32)
                    for k in range(3):
                        t = flux[a, b, k, row, ys, ls].astype(F32) * other
                        total[k] = total[k] + t if sign > 0 else total[k] - t
                for k in range(3):
                    part[k, row, ys, ls] = total[k]

        goes = (has_prev, has_next)

        def sh_rows_copy(side):
            src, dst = ((2, 6), (4, 0))[side]
            return remote(
                sh.at[src:src + 2], sh.at[dst:dst + 2],
                shx_send.at[side], shx_recv.at[side], (i, c + 2 * (2 * side - 1)),
            )

        def sh_landed(slot, block):
            at = sh.at[2 * block:2 * block + 2, pl.ds(slot * cols, cols)]
            remote(at, at, sh_send.at[0], sh_recv.at[slot, block], (i, c)).wait_recv()

        def shift_rows():
            loads[2].wait()
            for slot in range(window):
                sh_landed(slot, 1)

                @pl.when(start_of(i) + slot != i)
                def _():
                    sh_landed(slot, 2)
            for side in range(2):
                @pl.when(goes[side])
                def _():
                    sh_rows_copy(side).start()

        loads[1].wait()
        give_copy(0).wait_recv()
        whole_terms(2)
        for d in range(1, n_inst):
            y_copy(0, d).start()
        own_terms(3, 3, -1)
        give_copy(1).wait_recv()
        whole_terms(1)
        for d in range(1, n_inst):
            y_copy(1, d).start()
        give_copy(2).wait_recv()
        own_terms(0, 2, 1)
        heard(0)
        hello(1)

        for h in range(halves):
            @pl.when(has_prev)
            def _():
                halo_copy(0, h).wait_recv()
            halo_terms(0, 0, -1, h)
            for d in range(1, n_inst):
                y_copy(2 + 2 * h, d).start()

            @pl.when(has_next)
            def _():
                halo_copy(1, h).wait_recv()
            halo_terms(3, 5, 1, h)
            for d in range(1, n_inst):
                y_copy(3 + 2 * h, d).start()
            if h == 0:
                shift_rows()

        my_at = pl.multiple_of(start_of(i) * cols, cols)

        def add_up(piece):
            for d in range(1, n_inst):
                y_copy(piece, d).wait_recv()
            if piece < 2:
                row, ls = 2 - piece, slice(None)
            else:
                row, ls = (0, 3)[piece % 2], lanes(piece // 2 - 1)
            for k in range(3):
                total = part[k, row, pl.ds(my_at, wy), ls]
                for d in range(1, n_inst):
                    total = total + got[d - 1, k, row, :, ls]
                u0[k, ROW_A + row, :, ls] = total

        inner_moves = (
            (5, 1, 1, has_next),
            (5, 9, -1, has_prev),
            (4, 8, -1, has_prev),
            (4, 0, 1, has_next),
        )

        def in_copy(number):
            src, dst, dm, _ = inner_moves[number]
            return remote(
                u0.at[:, src], u0.at[:, dst], in_send.at[number], in_recv.at[number], (i, c + 2 * dm)
            )

        def in_start(number):
            @pl.when(inner_moves[number][3])
            def _():
                in_copy(number).start()

        def in_wait(number):
            arrives = has_prev if inner_moves[number][2] == 1 else has_next

            @pl.when(arrives)
            def _():
                in_copy(number).wait_recv()

        def x_copy(side, h):
            src, dst, dm = ((ROW_A, 7, -1), (ROW_D, 2, 1))[side]
            return remote(
                u0.at[:, src, :, lanes(h)], u0.at[:, dst, :, lanes(h)],
                x_send.at[side, h], x_recv.at[side, h], (i, c + 2 * dm),
            )

        add_up(0)
        in_start(0)
        in_start(1)
        add_up(1)
        in_start(2)
        for h in range(halves):
            for side in range(2):
                add_up(2 + 2 * h + side)

                @pl.when(goes[side])
                def _():
                    x_copy(side, h).start()

        heard(1)
        hello(2)

        shape = (wy, nz)
        y_at = lax.broadcasted_iota(jnp.int32, shape, 0)

        def valid_row(row):
            if row in PAIR_ROWS:
                return True
            return has_prev if row < ROW_A else has_next

        fields = (u0, u1, u2, u3)
        lane = lax.broadcasted_iota(jnp.int32, (1, 128), 1)

        def moment(n):
            total = energy(u2, sh) if n == 5 else None
            a, b = fields[n // 2], fields[(n + 1) // 2]
            for k in range(3 if n < 5 else 0):
                for row in PAIR_ROWS:
                    term = a[k, row] * b[k, row]
                    total = term if total is None else total + term
            if split:
                total = jnp.where((y_at >= own_at) & (y_at < own_at + cols), total, 0.0)
            value = jnp.sum(jnp.sum(total, axis=0, keepdims=True), axis=1, keepdims=True)
            return jnp.where(lane == n, value, 0.0)

        def arrived(side):
            there = goes[side]
            in_wait(0) if side == 0 else (in_wait(1), in_wait(2))

            @pl.when(there)
            def _():
                sh_rows_copy(1 - side).wait_recv()
                for h in range(halves):
                    x_copy(1 - side, h).wait_recv()

        apply_operator(u0, u1, sh, (4, 5), valid_row)
        pack[...] = moment(0)
        arrived(1)
        apply_operator(u0, u1, sh, (6, 7, 8), valid_row)
        apply_operator(u1, u2, sh, (6, 7), valid_row)
        arrived(0)
        in_start(3)
        apply_operator(u0, u1, sh, (2, 3), valid_row)
        apply_operator(u1, u2, sh, (3, 4, 5), valid_row)

        pack[...] += moment(1) + moment(2) + moment(3) + moment(4) + moment(5)
        for number in range(2, len(reaches)):
            heard(number)
            hello(number + 1)
        cores = (1,) if split else (0, 1)
        for to in range(n_pair):
            for core in cores:
                if core == 0:
                    moment_copy(to, core).start()
                else:
                    @pl.when(m != to)
                    def _():
                        moment_copy(to, core).start()
        for j in range(3):
            basis_copy(j).start()
        in_wait(3)
        apply_operator(u0, u1, sh, (1,), valid_row)
        apply_operator(u1, u2, sh, (2,), valid_row)
        apply_operator(u2, u3, sh, PAIR_ROWS, valid_row)
        basis_copy(3).start()

        for j in range(4):
            basis[j] = fields[j][:, ROW_C:ROW_C + 2, own]
        total = pack[...]
        for pair in range(n_pair):
            @pl.when(m != pair)
            def _():
                moment_from(pair).wait_recv()
            total = total + jnp.where(m != pair, gath[pair], 0.0)
        if split:
            pack2[...] = total
            for d in range(n_inst):
                for core in (0, 1):
                    if d > 0 or core == 0:
                        across_copy(d, core).start()
            for d in range(1, n_inst):
                across_copy(d, 1).wait_recv()
                total = total + gath2[d]
        sums[...] = total

        for j in range(4):
            basis_copy(j).wait_send()
        for to in range(n_pair):
            for core in cores:
                if core == 0:
                    moment_copy(to, core).wait_send()
                else:
                    @pl.when(m != to)
                    def _():
                        moment_copy(to, core).wait_send()
        if split:
            for d in range(n_inst):
                for core in (0, 1):
                    if d > 0 or core == 0:
                        across_copy(d, core).wait_send()
        for number in range(4):
            @pl.when(inner_moves[number][3])
            def _():
                in_copy(number).wait_send()
        for h in range(halves):
            for side in range(2):
                @pl.when(goes[side])
                def _():
                    x_copy(side, h).wait_send()

            @pl.when(has_next)
            def _():
                halo_copy(0, h).wait_send()
        for piece in range(2 + 2 * halves):
            for d in range(1, n_inst):
                y_copy(piece, d).wait_send()
        for dj in offsets:
            if dj != 0:
                @pl.when(reads_me(dj))
                def _():
                    sh_copy(dj, 2, 0).wait_send()
        for side in range(2):
            @pl.when(goes[side])
            def _():
                sh_rows_copy(side).wait_send()


def combine(basis, sums, x_out, r_out, x, r, sem):
    lane = lax.broadcasted_iota(jnp.int32, sums.shape, 1)
    mu = [
        jnp.sum(jnp.where(lane == m, sums[...], 0.0), axis=1, keepdims=True) for m in range(6)
    ]
    at_x, at_r = coefficients(mu)
    moves = []
    for k in range(3):
        b = [basis[j, k] for j in range(4)]
        x[k] = at_x[0] * b[0] + at_x[1] * b[1] + at_x[2] * b[2]
        r[k] = at_r[0] * b[0] + at_r[1] * b[1] + at_r[2] * b[2] + at_r[3] * b[3]
        for q, (src, dst) in enumerate(((x, x_out), (r, r_out))):
            moves.append(pltpu.make_async_copy(src.at[k], dst.at[k], sem.at[q, k]))
            moves[-1].start()
    for move in moves:
        move.wait()


def local(n_inst, n_cell, adjoint, flux_jac, shift):
    rows, cols, nz = shift.shape
    n_i, n_v, _, ny, _ = adjoint.shape
    window = min(3, n_inst)
    wy = window * cols
    n_pair = n_cell // 2
    field = pltpu.VMEM((3, 2 * rows + 2 * HALO, wy, nz), F32)
    dma = pltpu.SemaphoreType.DMA
    out = jax.ShapeDtypeStruct((3, rows, cols, nz), F32)
    peers = max(n_inst - 1, 1)
    answers = pl.pallas_call(
        functools.partial(kernel, n_inst, n_cell, cols, window),
        out_shape=(
            jax.ShapeDtypeStruct((4, 3, rows, cols, nz), F32),
            jax.ShapeDtypeStruct((1, 128), F32),
        ),
        in_specs=[pl.BlockSpec(memory_space=pltpu.HBM)] * 3,
        out_specs=(pl.BlockSpec(memory_space=pltpu.VMEM),) * 2,
        scratch_shapes=[
            pltpu.VMEM((n_i, n_v, 2 * rows + 2, ny, nz), adjoint.dtype),
            pltpu.VMEM((n_i, n_v, 3, 2 * rows, ny, nz), flux_jac.dtype),
            pltpu.VMEM((3, 2 * rows, ny, nz), F32),
            pltpu.VMEM((peers, 3, 2 * rows, wy, nz), F32),
            field, field, field, field,
            pltpu.VMEM((2 * rows + 4, wy, nz), F32),
            pltpu.VMEM((1, 128), F32),
            pltpu.VMEM((n_pair, 1, 128), F32),
            pltpu.VMEM((1, 128), F32),
            pltpu.VMEM((n_inst, 1, 128), F32),
            dma((3,)),
            dma((3,)), dma((3,)),
            dma((2,)), dma((2, 2)),
            dma((2 * window - 1,)), dma((window, 3)),
            dma((peers, 6)), dma((peers, 6)),
            dma((4,)), dma((4,)),
            dma((2, 2)), dma((2, 2)),
            dma((4,)), dma((4,)),
            dma((n_pair, 2)), dma((n_pair,)),
            dma((n_inst, 2)), dma((n_inst,)),
            pltpu.SemaphoreType.REGULAR((7,)),
            dma((2,)), dma((2,)),
        ],
        compiler_params=pltpu.CompilerParams(
            collective_id=0, has_side_effects=True, vmem_limit_bytes=VMEM_GRANT
        ),
    )(*[pltpu.with_memory_space_constraint(a, pltpu.HBM) for a in (adjoint, flux_jac, shift)])
    return pl.pallas_call(
        combine,
        out_shape=(out, out),
        in_specs=[pl.BlockSpec(memory_space=pltpu.VMEM)] * 2,
        out_specs=(pl.BlockSpec(memory_space=pltpu.HBM),) * 2,
        scratch_shapes=[
            pltpu.VMEM((3, rows, cols, nz), F32), pltpu.VMEM((3, rows, cols, nz), F32), dma((2, 3)),
        ],
        compiler_params=pltpu.CompilerParams(vmem_limit_bytes=2 << 20),
    )(*answers)


def solution(mesh):
    placed = (
        P("inst", None, "cell", None, None),
        P("inst", None, None, "cell", None, None),
        P("cell", "inst", None),
    )
    return jax.shard_map(
        functools.partial(local, mesh.shape["inst"], mesh.shape["cell"]),
        mesh=mesh,
        in_specs=placed,
        out_specs=(P(None, "cell", "inst", None), P(None, "cell", "inst", None)),
        check_vma=False,
    )
```
